32 devices in a mesh: heads: 4 (over y, core), seq: 8 (over z, x).
Axes of the slice: x: 2, y: 2, z: 4, core: 2. Of those that a mesh axis runs over, the one named last changes fastest.
Arguments:
- queries: bfloat16 [1024, 64, 576], P('seq', 'heads'), may hold values from -6 to 6
- latents: bfloat16 [8, 128, 576], P('seq', 'heads'), may hold values from -6 to 6
- grad_out: bfloat16 [1024, 64, 512], P('seq', 'heads'), may hold values from -6 to 6
- selected: int32 [8, 4], P('seq'), may hold values from 0 to 7, as said below
Outputs:
- output: bfloat16 [1024, 64, 512], P('seq', 'heads')
- grad_query: bfloat16 [1024, 64, 576], P('seq', 'heads')
- latent_grad: float32 [8, 128, 576], P('seq', 'heads')
The draws below stay inside these ranges and needn't reach their ends.
Inputs may be any that keep to these rules, and one draw needn't show every extreme that they name: `selected`: row i lists 4 different blocks, none of them held on the same index of seq as block i (blocks i and j share it when i // 1 equals j // 1); how often a block is chosen varies widely between blocks.
All inputs are finite; a program needn't handle non-finite values.
Results may differ from the reference program's by a relative error of at most 0.012.
Values may be sent and summed in bfloat16 or wider, within the bound.
A program may use at most 64 MiB of HBM per device.

```python
import jax
import jax.numpy as jnp
from jax import lax

HEADS = 64
LATENT = 512
BLOCK = 128
TOP = 4
DK = 576
QUERY_BLOCK_UNIT = 1
SEQ = 1024
NBLK = 8


def draw_latents(key, part):
    values = jnp.clip(jax.random.normal(jax.random.fold_in(key, 11), (NBLK, BLOCK, DK), jnp.float32), -6.0, 6.0)
    return values.astype(jnp.bfloat16)


def draw_queries(key, part):
    values = jnp.clip(jax.random.normal(jax.random.fold_in(key, 12), (SEQ, HEADS, DK), jnp.float32), -6.0, 6.0)
    return values.astype(jnp.bfloat16)


def draw_selected(key, part):
    popular = jax.random.randint(jax.random.fold_in(key, 21), (NBLK,), 0, 5)
    weight = (popular + 1) * (popular + 1)
    noise = jax.random.randint(jax.random.fold_in(key, 22), (NBLK, NBLK), 0, 4096)
    column_span = jnp.arange(NBLK, dtype=jnp.int32)
    scores = noise * weight[None, :] * NBLK + column_span[None, :]
    holder = column_span // QUERY_BLOCK_UNIT
    scores = jnp.where(holder[:, None] == holder[None, :], -1, scores)
    _, chosen = lax.top_k(scores, TOP)
    return chosen.astype(jnp.int32)


def levels(key, shape, split, smallest, top_value):
    loudness, own = 1.0, jax.random.fold_in(key, 6)
    for axis_at, shards_of in split:
        steps = jnp.exp(jax.random.uniform(jax.random.fold_in(own, axis_at), (shards_of,), jnp.float32, smallest / len(split), top_value / len(split)))
        loudness = loudness * jnp.repeat(steps, shape[axis_at] // shards_of).reshape([-1 if axis == axis_at else 1 for axis in range(len(shape))])
    return loudness


def scatter_about(key, shape, spread, bound, shards=(), kind=jnp.bfloat16):
    array = spread * jax.random.normal(key, shape, jnp.float32)
    if shards:
        array = array * levels(key, shape, shards, -0.22, 0.18)
    return jnp.clip(array, -bound, bound).astype(kind)


def setup_inputs(seed: int = 0) -> dict:
    arg_keys = jax.random.split(jax.random.key(seed), 5)
    return {
        "queries": draw_queries(jax.random.fold_in(arg_keys[4], 71), 0),
        "latents": draw_latents(jax.random.fold_in(arg_keys[4], 71), 0),
        "grad_out": scatter_about(arg_keys[2], (SEQ, HEADS, LATENT), 1.0, 6.0, ((0, 8), (1, 4))),
        "selected": draw_selected(jax.random.fold_in(arg_keys[4], 71), 0),
    }


def reference(queries, latents, grad_out, selected):
    list_blocks, block_size, key_width = latents.shape
    token_total, head_count, _ = queries.shape
    value_width = grad_out.shape[2]
    score_scale = key_width ** -0.5
    query_blocks = queries.reshape(list_blocks, block_size, head_count, key_width)
    grad_blocks = grad_out.reshape(list_blocks, block_size, head_count, value_width)
    own_blocks = jnp.arange(list_blocks, dtype=jnp.int32)[:, None]
    block_ids = jnp.concatenate([own_blocks, selected.astype(jnp.int32)], axis=1)

    def block_step(totals, pieces):
        query_row_tiles, grad_rows, key_ids = pieces
        key_row_tiles = latents[key_ids].reshape(-1, key_width).astype(jnp.float32)
        query_full = query_row_tiles.astype(jnp.float32)
        grad_full = grad_rows.astype(jnp.float32)
        value_rows = key_row_tiles[:, :value_width]
        scores = jnp.einsum('thd,kd->htk', query_full, key_row_tiles) * score_scale
        prob_full = jax.nn.softmax(scores, axis=-1)
        prob_half = prob_full.astype(jnp.bfloat16)
        output = jnp.einsum('htk,kl->thl', prob_half.astype(jnp.float32), value_rows).astype(jnp.bfloat16)
        row_delta = jnp.sum(grad_full * output.astype(jnp.float32), axis=-1)
        grad_prob = jnp.einsum('thl,kl->htk', grad_full, value_rows)
        score_gradient = (prob_full * (grad_prob - row_delta.T[:, :, None]) * score_scale).astype(jnp.bfloat16)
        grad_query = jnp.einsum('htk,kd->thd', score_gradient.astype(jnp.float32), key_row_tiles).astype(jnp.bfloat16)
        key_gradient = jnp.einsum('htk,thd->kd', score_gradient.astype(jnp.float32), query_full)
        grad_value = jnp.einsum('htk,thl->kl', prob_half.astype(jnp.float32), grad_full)
        key_gradient = key_gradient.at[:, :value_width].add(grad_value)
        totals = totals.at[key_ids].add(key_gradient.reshape(-1, block_size, key_width))
        return totals, (output, grad_query)

    start_grad = jnp.zeros((list_blocks, block_size, key_width), jnp.float32)
    latent_grad, (output, grad_query) = lax.scan(block_step, start_grad, (query_blocks, grad_blocks, block_ids))
    return (output.reshape(token_total, head_count, value_width),
            grad_query.reshape(token_total, head_count, key_width),
            latent_grad)
```

```python
import functools

import jax
import jax.numpy as jnp
from jax import lax
from jax.experimental import pallas as pl
from jax.experimental.pallas import tpu as pltpu
from jax.sharding import PartitionSpec as P

MESH = pl.DeviceIdType.MESH
VMEM = pltpu.MemorySpace.VMEM
SMEM = pltpu.MemorySpace.SMEM
HBM = pltpu.MemorySpace.HBM


def place(dims):
    a_n, b_n, g_n, c_n = dims
    s, h = lax.axis_index("seq"), lax.axis_index("heads")
    return s // b_n, lax.rem(s, b_n), h // c_n, lax.rem(h, c_n)


def other(x, k, n):
    return lax.rem(x + k, n)


def along(x, k, n):
    if n & (n - 1):
        return lax.rem(x + k, n)
    bit = 1
    while bit < n:
        x = x + bit * ((k // bit) % 2) * (1 - 2 * ((x // bit) % 2))
        bit *= 2
    return x


def looped(start, stop, fn, backwards=False):
    if stop - start <= 8:
        for k in reversed(range(start, stop)) if backwards else range(start, stop):
            fn(k)
    else:
        lax.fori_loop(start, stop, lambda k, _: (fn(k), 0)[1], 0)


def hail(dims, me):
    a_n, b_n, g_n, c_n = dims
    a, b, g, c = me
    barrier = pltpu.get_barrier_semaphore()

    def signal(a2, b2, g2, c2):
        pl.semaphore_signal(
            barrier, inc=1, device_id=(g2 * c_n + c2, a2 * b_n + b2), device_id_type=MESH
        )

    for k in range(1, c_n):
        signal(a, b, g, other(c, k, c_n))
    for k in range(1, b_n):
        signal(a, other(b, k, b_n), g, c)
    for k in range(1, g_n):
        signal(a, b, other(g, k, g_n), c)
    for k in range(1, a_n):
        signal(other(a, k, a_n), b, g, c)


def meet(dims):
    a_n, b_n, g_n, c_n = dims
    pl.semaphore_wait(pltpu.get_barrier_semaphore(), a_n + b_n + g_n + c_n - 4)


def gather(
    dims, own_ref, g_ref, q_ref, sel_ref, out_ref, g_out, q_out, near_ref, near,
    g_raw, g_in_sem, q_in_sem, own_sem, a_sem, b_sem, g_sem, c_sem, recv_sem, near_sem,
):
    a_n, b_n, g_n, c_n = dims
    me = place(dims)
    a, b, g, c = me
    hail(dims, me)
    mine = pltpu.make_async_copy(own_ref.at[0], out_ref.at[a * b_n + b, g * c_n + c], own_sem)
    mine.start()
    staged = pltpu.make_async_copy(g_ref, g_raw, g_in_sem)
    staged.start()
    heads, _, tokens = q_ref.shape
    across = [
        pltpu.make_async_copy(
            q_ref.at[h], q_out.at[:, h * tokens : (h + 1) * tokens], q_in_sem.at[h]
        )
        for h in range(heads)
    ]
    for cp in across:
        cp.start()
    meet(dims)
    asked = [
        pltpu.make_async_remote_copy(
            src_ref=sel_ref,
            dst_ref=near_ref.at[n],
            send_sem=near_sem.at[0, n],
            recv_sem=near_sem.at[1, n],
            device_id=(g * c_n + c, a * b_n + other(b, n, b_n)),
            device_id_type=MESH,
        )
        for n in range(1, b_n)
    ]

    swap = b_n == g_n
    flip = lax.rem(c, 2) if swap else 0

    def spot(ka, kp, kq, kc):
        kb, kg = (flip * kp + (1 - flip) * kq, (1 - flip) * kp + flip * kq) if swap else (kq, kp)
        return along(a, ka, a_n), other(b, kb, b_n), other(g, kg, g_n), other(c, kc, c_n)

    p_n, q_n = g_n, b_n

    def copy(key, step, sem, own):
        a1, b1, g1, c1 = spot(*key)
        a2, b2, g2, c2 = spot(*step)
        slot = (a1 * b_n + b1, g1 * c_n + c1)
        return pltpu.make_async_remote_copy(
            src_ref=own_ref.at[0] if own else out_ref.at[slot],
            dst_ref=out_ref.at[slot],
            send_sem=sem,
            recv_sem=recv_sem.at[slot],
            device_id=(g2 * c_n + c2, a2 * b_n + b2),
            device_id_type=MESH,
        )

    def arrived(*key):
        copy(key, (0, 0, 0, 0), own_sem, False).wait_recv()

    def sends(ka, kp, kq, own=False):
        key = (ka, kp, kq, 0)
        out = []
        if isinstance(kp, int) and kp == 0 and isinstance(kq, int) and kq == 0:
            out += [copy(key, (0, n, 0, 0), b_sem.at[ka, n], own) for n in range(1, p_n)]
        if isinstance(kq, int) and kq == 0:
            out += [copy(key, (0, 0, n, 0), g_sem.at[ka * p_n + kp, n], own) for n in range(1, q_n)]
        out += [
            copy(key, (0, 0, 0, n), c_sem.at[ka * p_n + kp, kq, n], own) for n in range(1, c_n)
        ]
        return out

    def firsts():
        return [copy((0, 0, 0, 0), (n, 0, 0, 0), a_sem.at[n], True) for n in range(1, a_n)]

    def over_a(fn):
        if a_n <= 8:
            for ka in range(1, a_n):
                fn(ka)
        elif a_n > 1:
            lax.fori_loop(1, a_n, lambda ka, _: (fn(ka), 0)[1], 0)

    def relay(ka, kp, kq):
        arrived(ka, kp, kq, 0)
        for cp in sends(ka, kp, kq):
            cp.start()

    for cp in firsts() + sends(0, 0, 0, True) + asked:
        cp.start()
    staged.wait()
    g_out[...] = jnp.swapaxes(g_raw[...], 0, 1)
    for kp in range(1, p_n):
        relay(0, kp, 0)
    for kq in range(1, q_n):
        relay(0, 0, kq)
    over_a(lambda ka: relay(ka, 0, 0))
    for kp in range(1, p_n):
        for kq in range(1, q_n):
            relay(0, kp, kq)
    over_a(lambda ka: [relay(ka, kp, 0) for kp in range(1, p_n)])
    over_a(lambda ka: [relay(ka, 0, kq) for kq in range(1, q_n)])
    over_a(lambda ka: [relay(ka, kp, kq) for kp in range(1, p_n) for kq in range(1, q_n)])

    def finish(ka):
        for kp in range(p_n):
            for kq in range(q_n):
                for kc in range(1, c_n):
                    arrived(ka, kp, kq, kc)
                for cp in sends(ka, kp, kq):
                    cp.wait_send()

    finish(0)
    over_a(finish)
    for cp in firsts():
        cp.wait_send()
    mine.wait()
    for cp in asked:
        cp.wait()
    for n in range(1, b_n):
        noted = pltpu.make_async_copy(near_ref.at[n], near.at[n], near_sem.at[0, 0])
        noted.start()
        noted.wait()
    for cp in across:
        cp.wait()


def attend(
    dims, scale, width, sel_ref, near_ref, all_ref, q_ref, g_ref, o_ref, dq_ref, out_ref,
    keys, keys_t, probs, grads, o_rows, con, c_in, g_out, g_in, sums, x_out, x_in, z_out, z_in,
    c_sem, g_sem, x_sem, z_sem,
):
    a_n, b_n, g_n, c_n = dims
    me = place(dims)
    a, b, g, c = me
    count = sel_ref.shape[1] + 1
    heads, tokens, value_width = g_ref.shape
    key_width, columns = q_ref.shape
    rows = all_ref.shape[2]
    block = rows * g_n * c_n
    f32, bf16 = jnp.float32, jnp.bfloat16
    across = (((1,), (1,)), ((), ()))
    down = (((0,), (0,)), ((), ()))

    def copy(src, dst, sems, there):
        a2, b2, g2, c2 = there
        return pltpu.make_async_remote_copy(
            src_ref=src,
            dst_ref=dst,
            send_sem=sems.at[0],
            recv_sem=sems.at[1],
            device_id=(g2 * c_n + c2, a2 * b_n + b2),
            device_id_type=MESH,
        )

    def to_c(p, k):
        c2 = other(c, k, c_n)
        return copy(con.at[p, :, c2], c_in.at[p, k], c_sem.at[p, k], (a, b, g, c2))

    def to_g(p, k):
        return copy(g_out.at[p, k], g_in.at[p, k], g_sem.at[p, k], (a, b, other(g, k, g_n), c))

    def to_x(p, k):
        return copy(x_out.at[p], x_in.at[k, p], x_sem.at[p, k], (a, other(b, k, b_n), g, c))

    def to_z(k):
        return copy(z_out.at[k], z_in.at[k], z_sem.at[k], (along(a, k, a_n), b, g, c))

    sums[0] = jnp.zeros(sums.shape[1:], f32)
    for k in range(1, b_n):
        x_in[k, 0] = jnp.zeros(x_in.shape[2:], bf16)

    for n in range(count):
        at = lax.axis_index("seq") if n == 0 else sel_ref[0, n - 1]
        keys[n * block : (n + 1) * block, :] = all_ref[at].reshape(block, key_width)

    def rows_of(n):
        return g_ref[n // tokens : (n + width) // tokens].reshape(width, value_width)

    for n in range(0, columns, width):
        scores = jnp.dot(keys[...], q_ref[:, n : n + width], preferred_element_type=f32)
        top = jnp.max(scores, axis=0, keepdims=True)
        weights = jnp.exp((scores - top) * scale)
        norm = 1.0 / jnp.sum(weights, axis=0, keepdims=True)
        grad_prob = lax.dot_general(
            keys[:, :value_width], rows_of(n), across, preferred_element_type=f32
        )
        delta = jnp.sum(weights * grad_prob, axis=0, keepdims=True) * norm
        probs[:, n : n + width] = (weights * norm).astype(bf16)
        grads[:, n : n + width] = (weights * (norm * scale) * (grad_prob - delta)).astype(bf16)

    def contribute(first, last):
        at = slice(first * block, last * block)
        total = lax.dot_general(grads[at, :], q_ref[...], across, preferred_element_type=f32)
        value = jnp.dot(
            probs[at, :], g_ref[...].reshape(columns, value_width), preferred_element_type=f32
        )
        total = jnp.concatenate([total[:, :value_width] + value, total[:, value_width:]], axis=1)
        con[first:last] = total.astype(bf16).reshape(last - first, g_n, c_n, rows, key_width)
        for p in range(first, last):
            for k in range(1, c_n):
                to_c(p, k).start()

    def chip_sum(p, g1):
        total = con[p, g1, c].astype(f32)
        for k in range(1, c_n):
            total += c_in[p, k, g1].astype(f32)
        return total

    def to_groups(p):
        for k in range(1, c_n):
            to_c(p, k).wait_recv()
        for k in range(1, g_n):
            g_out[p, k] = chip_sum(p, other(g, k, g_n)).astype(bf16)
            to_g(p, k).start()

    def head_sum(p):
        total = chip_sum(p, g)
        for k in range(1, g_n):
            to_g(p, k).wait_recv()
            total += g_in[p, k].astype(f32)
        return total

    def to_row(p):
        total = head_sum(p)
        sums[p] = total
        x_out[p] = total.astype(bf16)
        for k in range(1, b_n):
            to_x(p, k).start()

    def outputs(n):
        o_rows[n : n + width, :] = lax.dot_general(
            probs[:, n : n + width], keys[:, :value_width], down, preferred_element_type=f32
        ).astype(bf16)
        dq = jnp.dot(keys_t[...], grads[:, n : n + width], preferred_element_type=f32).astype(bf16)
        for m in range(width // tokens):
            dq_ref[n // tokens + m] = dq[:, m * tokens : (m + 1) * tokens]

    pairs = [(p, min(p + 2, count)) for p in range(1, count, 2)]
    for n, pair in enumerate(pairs):
        contribute(*pair)
        for p in range(*pairs[n - 1]) if n else ():
            to_groups(p)
    for p in range(*pairs[-1]):
        to_groups(p)
    contribute(0, 1)
    keys_t[...] = keys[...].T
    starts = list(range(0, columns, width))
    cuts = [len(starts) * n // (count - 1) for n in range(count)]
    to_groups(0)
    for p in range(1, count):
        to_row(p)
        for n in starts[cuts[p - 1] : cuts[p]]:
            outputs(n)
    part = 8 if heads % 8 == 0 else heads
    for h in range(0, heads, part):
        o_ref[:, h : h + part, :] = jnp.swapaxes(
            o_rows[h * tokens : (h + part) * tokens, :].reshape(part, tokens, value_width), 0, 1
        )

    for k in range(1, b_n):
        for p in range(1, count):
            to_x(p, k).wait_recv()

    def slot(chosen, wanted):
        at = 0
        for p in range(1, count):
            at = jnp.where(chosen(p - 1) == wanted, p, at)
        return at

    def dense(a1):
        wanted = a1 * b_n + b
        total = sums[slot(lambda p: sel_ref[0, p], wanted)]
        for k in range(1, b_n):
            total += x_in[k, slot(lambda p: near_ref[k, 0, p], wanted)].astype(f32)
        return total

    def send_z(k):
        z_out[k] = dense(along(a, k, a_n)).astype(bf16)
        to_z(k).start()

    looped(1, a_n, send_z, True)
    out_ref[...] = dense(a) + head_sum(0)

    def take_z(k):
        to_z(k).wait_recv()
        out_ref[...] += z_in[k].astype(f32)

    looped(1, a_n, take_z)
    looped(1, a_n, lambda k: to_z(k).wait_send())
    for p in range(count):
        for k in range(1, c_n):
            to_c(p, k).wait_send()
        for k in range(1, g_n):
            to_g(p, k).wait_send()
        if p:
            for k in range(1, b_n):
                to_x(p, k).wait_send()


def layer_kernel(
    dims, scale, width, sel_ref, sel_raw, own_ref, q_raw, g_in, o_ref, dq_ref, out_ref,
    pieces, g_rows, q_cols, near_raw, near, *refs,
):
    gather(dims, own_ref, g_in, q_raw, sel_raw, pieces, g_rows, q_cols, near_raw, near, *refs[:10])
    attend(
        dims, scale, width, sel_ref, near, pieces, q_cols, g_rows, o_ref, dq_ref, out_ref,
        *refs[10:],
    )


def layer(selected, latents, queries, grad_out, dims):
    a_n, b_n, g_n, c_n = dims
    n_s, n_h = a_n * b_n, g_n * c_n
    heads, key_width, tokens = queries.shape
    value_width = grad_out.shape[2]
    columns = heads * tokens
    count = selected.shape[1] + 1
    rows = latents.shape[1]
    keys = count * rows * n_h
    one = (rows, key_width)
    dma = pltpu.SemaphoreType.DMA
    half = functools.partial(pltpu.VMEM, dtype=jnp.bfloat16)
    width = tokens * (4 if heads % 4 == 0 else 1)
    return pl.pallas_call(
        functools.partial(layer_kernel, dims, key_width ** (-0.5), width),
        out_shape=(
            half((tokens, heads, value_width)),
            half((heads, key_width, tokens)),
            pltpu.VMEM(one, jnp.float32),
        ),
        in_specs=[pl.BlockSpec(memory_space=SMEM)] + [pl.BlockSpec(memory_space=HBM)] * 4,
        out_specs=[pl.BlockSpec(memory_space=VMEM)] * 3,
        scratch_shapes=[
            half((n_s, n_h) + one),
            half((heads, tokens, value_width)),
            half((key_width, columns)),
            pltpu.VMEM((b_n,) + selected.shape, selected.dtype),
            SMEM((b_n,) + selected.shape, selected.dtype),
            half(grad_out.shape),
            dma,
            dma((heads,)),
            dma,
            dma((a_n,)),
            dma((a_n, g_n)),
            dma((a_n * g_n, b_n)),
            dma((a_n * g_n, b_n, c_n)),
            dma((n_s, n_h)),
            dma((2, b_n)),
            half((keys, key_width)),
            half((key_width, keys)),
            half((keys, columns)),
            half((keys, columns)),
            half((columns, value_width)),
            half((count, g_n, c_n) + one),
            half((count, c_n, g_n) + one),
            half((count, g_n) + one),
            half((count, g_n) + one),
            pltpu.VMEM((count,) + one, jnp.float32),
            half((count,) + one),
            half((b_n, count) + one),
            half((a_n,) + one),
            half((a_n,) + one),
            dma((count, c_n, 2)),
            dma((count, g_n, 2)),
            dma((count, b_n, 2)),
            dma((a_n, 2)),
        ],
        compiler_params=pltpu.CompilerParams(
            collective_id=0, has_side_effects=True, vmem_limit_bytes=67043328 - 5500000
        ),
        name="layer",
    )(selected, selected, latents, queries, grad_out)


def hand_out_kernel(*refs):
    n = (len(refs) - 1) // 2
    copies = [pltpu.make_async_copy(refs[k], refs[n + k], refs[-1].at[k]) for k in range(n)]
    for cp in copies:
        cp.start()
    for cp in copies:
        cp.wait()


def hand_out(arrays):
    return pl.pallas_call(
        hand_out_kernel,
        out_shape=[jax.ShapeDtypeStruct(x.shape, x.dtype) for x in arrays],
        in_specs=[pl.BlockSpec(memory_space=VMEM) for _ in arrays],
        out_specs=[pl.BlockSpec(memory_space=HBM) for _ in arrays],
        scratch_shapes=[pltpu.SemaphoreType.DMA((len(arrays),))],
        compiler_params=pltpu.CompilerParams(vmem_limit_bytes=16 * 1024 * 1024),
        name="hand_out",
    )(*arrays)


def shards(dims, queries, latents, grad_out, selected):
    assert latents.shape[0] == 1
    output, grad_query, latent_grad = hand_out(
        layer(selected, latents, jnp.transpose(queries, (1, 2, 0)), grad_out, dims)
    )
    return output, jnp.transpose(grad_query, (2, 0, 1)), latent_grad[None]


def solution(mesh):
    n_h, n_s = mesh.shape["heads"], mesh.shape["seq"]
    b_n = 2 if n_s % 2 == 0 else 1
    c_n = 2 if n_h % 2 == 0 else 1
    dims = (n_s // b_n, b_n, n_h // c_n, c_n)
    in_specs = (
        P("seq", "heads", None),
        P("seq", "heads", None),
        P("seq", "heads", None),
        P("seq", None),
    )
    out_specs = (P("seq", "heads", None), P("seq", "heads", None), P("seq", "heads", None))
    return jax.shard_map(
        functools.partial(shards, dims),
        mesh=mesh, in_specs=in_specs, out_specs=out_specs, check_vma=False,
    )
```

```python
import functools

import jax
import jax.numpy as jnp
from jax import lax
from jax.experimental import pallas as pl
from jax.experimental.pallas import tpu as pltpu
from jax.sharding import PartitionSpec as P

MESH = pl.DeviceIdType.MESH
VMEM = pltpu.MemorySpace.VMEM
SMEM = pltpu.MemorySpace.SMEM
HBM = pltpu.MemorySpace.HBM


def place(dims):
    a_n, b_n, g_n, c_n = dims
    s, h = lax.axis_index("seq"), lax.axis_index("heads")
    return s // b_n, lax.rem(s, b_n), h // c_n, lax.rem(h, c_n)


def other(x, k, n):
    return lax.rem(x + k, n)


def along(x, k, n):
    if n & (n - 1):
        return lax.rem(x + k, n)
    bit = 1
    while bit < n:
        x = x + bit * ((k // bit) % 2) * (1 - 2 * ((x // bit) % 2))
        bit *= 2
    return x


def looped(start, stop, fn, backwards=False):
    if stop - start <= 8:
        for k in reversed(range(start, stop)) if backwards else range(start, stop):
            fn(k)
    else:
        lax.fori_loop(start, stop, lambda k, _: (fn(k), 0)[1], 0)


def hail(dims, me):
    a_n, b_n, g_n, c_n = dims
    a, b, g, c = me
    barrier = pltpu.get_barrier_semaphore()

    def signal(a2, b2, g2, c2):
        pl.semaphore_signal(
            barrier, inc=1, device_id=(g2 * c_n + c2, a2 * b_n + b2), device_id_type=MESH
        )

    for k in range(1, c_n):
        signal(a, b, g, other(c, k, c_n))
    for k in range(b_n):
        for n in range(g_n):
            if k or n:
                signal(a, other(b, k, b_n), other(g, n, g_n), c)
    for k in range(1, a_n):
        signal(other(a, k, a_n), b, g, c)


def meet(dims):
    a_n, b_n, g_n, c_n = dims
    pl.semaphore_wait(pltpu.get_barrier_semaphore(), a_n + b_n * g_n + c_n - 3)


def gather(
    dims, own_ref, g_ref, q_ref, sel_ref, out_ref, g_out, q_out, near_ref, near,
    g_raw, g_in_sem, q_in_sem, own_sem, a_sem, b_sem, c_sem, recv_sem, near_sem,
):
    a_n, b_n, g_n, c_n = dims
    me = place(dims)
    a, b, g, c = me
    hail(dims, me)
    mine = pltpu.make_async_copy(own_ref.at[0], out_ref.at[a * b_n + b, g * c_n + c], own_sem)
    mine.start()
    staged = pltpu.make_async_copy(g_ref, g_raw, g_in_sem)
    staged.start()
    heads, _, tokens = q_ref.shape
    across = [
        pltpu.make_async_copy(
            q_ref.at[h], q_out.at[:, h * tokens : (h + 1) * tokens], q_in_sem.at[h]
        )
        for h in range(heads)
    ]
    for cp in across:
        cp.start()
    meet(dims)
    asked = [
        pltpu.make_async_remote_copy(
            src_ref=sel_ref,
            dst_ref=near_ref.at[n],
            send_sem=near_sem.at[0, n],
            recv_sem=near_sem.at[1, n],
            device_id=(g * c_n + c, a * b_n + other(b, n, b_n)),
            device_id_type=MESH,
        )
        for n in range(1, b_n)
    ]

    swap = b_n == g_n
    flip = lax.rem(c, 2) if swap else 0

    def spot(ka, kp, kq, kc):
        kb, kg = (flip * kp + (1 - flip) * kq, (1 - flip) * kp + flip * kq) if swap else (kq, kp)
        return along(a, ka, a_n), other(b, kb, b_n), other(g, kg, g_n), other(c, kc, c_n)

    p_n, q_n = g_n, b_n

    def copy(key, step, sem, own):
        a1, b1, g1, c1 = spot(*key)
        a2, b2, g2, c2 = spot(*step)
        slot = (a1 * b_n + b1, g1 * c_n + c1)
        return pltpu.make_async_remote_copy(
            src_ref=own_ref.at[0] if own else out_ref.at[slot],
            dst_ref=out_ref.at[slot],
            send_sem=sem,
            recv_sem=recv_sem.at[slot],
            device_id=(g2 * c_n + c2, a2 * b_n + b2),
            device_id_type=MESH,
        )

    def arrived(*key):
        copy(key, (0, 0, 0, 0), own_sem, False).wait_recv()

    def sends(ka, kp, kq, own=False):
        key = (ka, kp, kq, 0)
        out = []
        if isinstance(kp, int) and kp == 0 and isinstance(kq, int) and kq == 0:
            out += [
                copy(key, (0, m, n, 0), b_sem.at[ka, m, n], own)
                for m in range(p_n) for n in range(q_n) if m or n
            ]
        out += [
            copy(key, (0, 0, 0, n), c_sem.at[ka * p_n + kp, kq, n], own) for n in range(1, c_n)
        ]
        return out

    def firsts():
        return [copy((0, 0, 0, 0), (n, 0, 0, 0), a_sem.at[n], True) for n in range(1, a_n)]

    def over_a(fn):
        if a_n <= 8:
            for ka in range(1, a_n):
                fn(ka)
        elif a_n > 1:
            lax.fori_loop(1, a_n, lambda ka, _: (fn(ka), 0)[1], 0)

    def relay(ka, kp, kq):
        arrived(ka, kp, kq, 0)
        for cp in sends(ka, kp, kq):
            cp.start()

    for cp in firsts() + sends(0, 0, 0, True) + asked:
        cp.start()
    staged.wait()
    g_out[...] = jnp.swapaxes(g_raw[...], 0, 1)
    for kp in range(1, p_n):
        relay(0, kp, 0)
    for kq in range(1, q_n):
        relay(0, 0, kq)
    over_a(lambda ka: relay(ka, 0, 0))
    for kp in range(1, p_n):
        for kq in range(1, q_n):
            relay(0, kp, kq)
    over_a(lambda ka: [relay(ka, kp, 0) for kp in range(1, p_n)])
    over_a(lambda ka: [relay(ka, 0, kq) for kq in range(1, q_n)])
    over_a(lambda ka: [relay(ka, kp, kq) for kp in range(1, p_n) for kq in range(1, q_n)])

    def last(ka):
        for kp in range(p_n):
            for kq in range(q_n):
                for kc in range(1, c_n):
                    arrived(ka, kp, kq, kc)

    for cp in asked:
        cp.wait()
    for n in range(1, b_n):
        noted = pltpu.make_async_copy(near_ref.at[n], near.at[n], near_sem.at[0, 0])
        noted.start()
        noted.wait()
    for cp in across:
        cp.wait()
    mine.wait()
    last(0)
    over_a(last)

    def finish():
        def sent(ka):
            for kp in range(p_n):
                for kq in range(q_n):
                    for cp in sends(ka, kp, kq):
                        cp.wait_send()

        sent(0)
        over_a(sent)
        for cp in firsts():
            cp.wait_send()

    return finish


def attend(
    dims, scale, width, finish, sel_ref, near_ref, all_ref, q_ref, g_ref, o_ref, dq_ref, out_ref,
    keys, keys_t, probs, grads, o_rows, con, c_in, g_out, g_in, sums, x_out, z_out, z_in,
    c_sem, g_sem, x_sem, z_sem, *x_in,
):
    a_n, b_n, g_n, c_n = dims
    me = place(dims)
    a, b, g, c = me
    chosen = sel_ref.shape[1]
    heads, tokens, value_width = g_ref.shape
    key_width, columns = q_ref.shape
    strips, _, _, strip, _ = con.shape
    parts = strips // (chosen + 1)
    height = strip * g_n * c_n
    f32, bf16 = jnp.float32, jnp.bfloat16
    across = (((1,), (1,)), ((), ()))
    down = (((0,), (0,)), ((), ()))
    units = [(n * chosen, (n + 1) * chosen) for n in range(parts)] + [(parts * chosen, strips)]

    def copy(src, dst, sems, there):
        a2, b2, g2, c2 = there
        return pltpu.make_async_remote_copy(
            src_ref=src,
            dst_ref=dst,
            send_sem=sems.at[0],
            recv_sem=sems.at[1],
            device_id=(g2 * c_n + c2, a2 * b_n + b2),
            device_id_type=MESH,
        )

    def to_c(n, k):
        c2 = other(c, k, c_n)
        at = pl.ds(units[n][0], units[n][1] - units[n][0])
        return copy(con.at[at, :, c2], c_in.at[k, at], c_sem.at[n, k], (a, b, g, c2))

    def to_g(u, k):
        return copy(g_out.at[u, k], g_in.at[u, k], g_sem.at[u, k], (a, b, other(g, k, g_n), c))

    def to_x(u, k):
        h, p = divmod(u, chosen)
        return copy(x_out.at[u], x_in[h].at[k, p + 1], x_sem.at[u, k], (a, other(b, k, b_n), g, c))

    def to_z(h, k):
        return copy(z_out.at[h, k], z_in.at[h, k], z_sem.at[h, k], (along(a, k, a_n), b, g, c))

    for h in range(parts):
        sums[h, 0] = jnp.zeros(sums.shape[2:], f32)
        for k in range(1, b_n):
            x_in[h][k, 0] = jnp.zeros(x_in[h].shape[2:], bf16)

    for p in range(-1, chosen):
        at = lax.axis_index("seq") if p < 0 else sel_ref[0, p]
        for h in range(parts):
            u = parts * chosen + h if p < 0 else h * chosen + p
            keys[u * height : (u + 1) * height, :] = all_ref[
                at, :, h * strip : (h + 1) * strip, :
            ].reshape(height, key_width)

    def rows_of(n):
        return g_ref[n // tokens : (n + width) // tokens].reshape(width, value_width)

    for n in range(0, columns, width):
        scores = jnp.dot(keys[...], q_ref[:, n : n + width], preferred_element_type=f32)
        top = jnp.max(scores, axis=0, keepdims=True)
        weights = jnp.exp((scores - top) * scale)
        norm = 1.0 / jnp.sum(weights, axis=0, keepdims=True)
        grad_prob = lax.dot_general(
            keys[:, :value_width], rows_of(n), across, preferred_element_type=f32
        )
        delta = jnp.sum(weights * grad_prob, axis=0, keepdims=True) * norm
        probs[:, n : n + width] = (weights * norm).astype(bf16)
        grads[:, n : n + width] = (weights * (norm * scale) * (grad_prob - delta)).astype(bf16)

    def contribute(n):
        first, last = units[n]
        at = slice(first * height, last * height)
        total = lax.dot_general(grads[at, :], q_ref[...], across, preferred_element_type=f32)
        value = jnp.dot(
            probs[at, :], g_ref[...].reshape(columns, value_width), preferred_element_type=f32
        )
        total = jnp.concatenate([total[:, :value_width] + value, total[:, value_width:]], axis=1)
        con[first:last] = total.astype(bf16).reshape(last - first, g_n, c_n, strip, key_width)
        for k in range(1, c_n):
            to_c(n, k).start()

    def chip_sum(u, g1):
        total = con[u, g1, c].astype(f32)
        for k in range(1, c_n):
            total += c_in[k, u, g1].astype(f32)
        return total

    def to_groups(n):
        for k in range(1, c_n):
            to_c(n, k).wait_recv()
        for u in range(*units[n]):
            for k in range(1, g_n):
                g_out[u, k] = chip_sum(u, other(g, k, g_n)).astype(bf16)
                to_g(u, k).start()

    def head_sum(u):
        total = chip_sum(u, g)
        for k in range(1, g_n):
            to_g(u, k).wait_recv()
            total += g_in[u, k].astype(f32)
        return total

    def to_row(n):
        for u in range(*units[n]):
            total = head_sum(u)
            sums[n, u % chosen + 1] = total
            x_out[u] = total.astype(bf16)
            for k in range(1, b_n):
                to_x(u, k).start()

    def outputs(n):
        o_rows[n : n + width, :] = lax.dot_general(
            probs[:, n : n + width], keys[:, :value_width], down, preferred_element_type=f32
        ).astype(bf16)
        dq = jnp.dot(keys_t[...], grads[:, n : n + width], preferred_element_type=f32).astype(bf16)
        for m in range(width // tokens):
            dq_ref[n // tokens + m] = dq[:, m * tokens : (m + 1) * tokens]

    def slot(row, wanted):
        at = 0
        for p in range(chosen):
            at = jnp.where(row(p) == wanted, p + 1, at)
        return at

    def dense(h, a1):
        wanted = a1 * b_n + b
        total = sums[h, slot(lambda p: sel_ref[0, p], wanted)]
        for k in range(1, b_n):
            total += x_in[h][k, slot(lambda p: near_ref[k, 0, p], wanted)].astype(f32)
        return total

    def to_holders(h):
        for k in range(1, b_n):
            for u in range(*units[h]):
                to_x(u, k).wait_recv()

        def send(k):
            z_out[h, k] = dense(h, along(a, k, a_n)).astype(bf16)
            to_z(h, k).start()

        looped(1, a_n, send, True)
        out_ref[h * strip : (h + 1) * strip, :] = dense(h, a)

    own = parts
    for n in range(parts):
        contribute(n)
        if n:
            to_groups(n - 1)
    contribute(own)
    to_groups(parts - 1)
    keys_t[...] = keys[...].T
    starts = list(range(0, columns, width))
    spans = 2 * parts
    cuts = [len(starts) * n // spans for n in range(spans + 1)]
    for n in range(spans):
        if n < parts:
            to_row(n)
        else:
            to_holders(n - parts)
        for m in starts[cuts[n] : cuts[n + 1]]:
            outputs(m)
        if n == 0:
            to_groups(own)
    part = 8 if heads % 8 == 0 else heads
    for h in range(0, heads, part):
        o_ref[:, h : h + part, :] = jnp.swapaxes(
            o_rows[h * tokens : (h + part) * tokens, :].reshape(part, tokens, value_width), 0, 1
        )
    for h in range(parts):
        out_ref[h * strip : (h + 1) * strip, :] += head_sum(units[own][0] + h)
    finish()
    for n in range(parts + 1):
        for k in range(1, c_n):
            to_c(n, k).wait_send()
    for u in range(strips):
        for k in range(1, g_n):
            to_g(u, k).wait_send()
        if u < parts * chosen:
            for k in range(1, b_n):
                to_x(u, k).wait_send()
    for h in range(parts):
        looped(1, a_n, lambda k: to_z(h, k).wait_send())

        def take(k):
            to_z(h, k).wait_recv()
            out_ref[h * strip : (h + 1) * strip, :] += z_in[h, k].astype(f32)

        looped(1, a_n, take)


def layer_kernel(
    dims, scale, width, sel_ref, sel_raw, own_ref, q_raw, g_in, o_ref, dq_ref, out_ref,
    pieces, g_rows, q_cols, near_raw, near, *refs,
):
    finish = gather(
        dims, own_ref, g_in, q_raw, sel_raw, pieces, g_rows, q_cols, near_raw, near, *refs[:9]
    )
    attend(
        dims, scale, width, finish, sel_ref, near, pieces, q_cols, g_rows, o_ref, dq_ref, out_ref,
        *refs[9:],
    )


def layer(selected, latents, queries, grad_out, dims):
    a_n, b_n, g_n, c_n = dims
    n_s, n_h = a_n * b_n, g_n * c_n
    heads, key_width, tokens = queries.shape
    value_width = grad_out.shape[2]
    columns = heads * tokens
    count = selected.shape[1] + 1
    rows = latents.shape[1]
    keys = count * rows * n_h
    one = (rows, key_width)
    parts = 2 if rows % 32 == 0 else 1
    strips = parts * count
    strip = (rows // parts, key_width)
    dma = pltpu.SemaphoreType.DMA
    half = functools.partial(pltpu.VMEM, dtype=jnp.bfloat16)
    width = tokens * (4 if heads % 4 == 0 else 1)
    return pl.pallas_call(
        functools.partial(layer_kernel, dims, key_width ** (-0.5), width),
        out_shape=(
            half((tokens, heads, value_width)),
            half((heads, key_width, tokens)),
            pltpu.VMEM(one, jnp.float32),
        ),
        in_specs=[pl.BlockSpec(memory_space=SMEM)] + [pl.BlockSpec(memory_space=HBM)] * 4,
        out_specs=[pl.BlockSpec(memory_space=VMEM)] * 3,
        scratch_shapes=[
            half((n_s, n_h) + one),
            half((heads, tokens, value_width)),
            half((key_width, columns)),
            pltpu.VMEM((b_n,) + selected.shape, selected.dtype),
            SMEM((b_n,) + selected.shape, selected.dtype),
            half(grad_out.shape),
            dma,
            dma((heads,)),
            dma,
            dma((a_n,)),
            dma((a_n, g_n, b_n)),
            dma((a_n * g_n, b_n, c_n)),
            dma((n_s, n_h)),
            dma((2, b_n)),
            half((keys, key_width)),
            half((key_width, keys)),
            half((keys, columns)),
            half((keys, columns)),
            half((columns, value_width)),
            half((strips, g_n, c_n) + strip),
            half((c_n, strips, g_n) + strip),
            half((strips, g_n) + strip),
            half((strips, g_n) + strip),
            pltpu.VMEM((parts, count) + strip, jnp.float32),
            half((strips,) + strip),
            half((parts, a_n) + strip),
            half((parts, a_n) + strip),
            dma((parts + 1, c_n, 2)),
            dma((strips, g_n, 2)),
            dma((strips, b_n, 2)),
            dma((parts, a_n, 2)),
        ] + [half((b_n, count) + strip)] * parts,
        compiler_params=pltpu.CompilerParams(
            collective_id=0, has_side_effects=True, vmem_limit_bytes=67043328 - 5500000
        ),
        name="layer",
    )(selected, selected, latents, queries, grad_out)


def hand_out_kernel(*refs):
    n = (len(refs) - 1) // 2
    copies = [pltpu.make_async_copy(refs[k], refs[n + k], refs[-1].at[k]) for k in range(n)]
    for cp in copies:
        cp.start()
    for cp in copies:
        cp.wait()


def hand_out(arrays):
    return pl.pallas_call(
        hand_out_kernel,
        out_shape=[jax.ShapeDtypeStruct(x.shape, x.dtype) for x in arrays],
        in_specs=[pl.BlockSpec(memory_space=VMEM) for _ in arrays],
        out_specs=[pl.BlockSpec(memory_space=HBM) for _ in arrays],
        scratch_shapes=[pltpu.SemaphoreType.DMA((len(arrays),))],
        compiler_params=pltpu.CompilerParams(vmem_limit_bytes=16 * 1024 * 1024),
        name="hand_out",
    )(*arrays)


def shards(dims, queries, latents, grad_out, selected):
    assert latents.shape[0] == 1
    output, grad_query, latent_grad = hand_out(
        layer(selected, latents, jnp.transpose(queries, (1, 2, 0)), grad_out, dims)
    )
    return output, jnp.transpose(grad_query, (2, 0, 1)), latent_grad[None]


def solution(mesh):
    n_h, n_s = mesh.shape["heads"], mesh.shape["seq"]
    b_n = 2 if n_s % 2 == 0 else 1
    c_n = 2 if n_h % 2 == 0 else 1
    dims = (n_s // b_n, b_n, n_h // c_n, c_n)
    in_specs = (
        P("seq", "heads", None),
        P("seq", "heads", None),
        P("seq", "heads", None),
        P("seq", None),
    )
    out_specs = (P("seq", "heads", None), P("seq", "heads", None), P("seq", "heads", None))
    return jax.shard_map(
        functools.partial(shards, dims),
        mesh=mesh, in_specs=in_specs, out_specs=out_specs, check_vma=False,
    )
```

```python
import functools

import jax
import jax.numpy as jnp
from jax import lax
from jax.experimental import pallas as pl
from jax.experimental.pallas import tpu as pltpu
from jax.sharding import PartitionSpec as P

MESH = pl.DeviceIdType.MESH
VMEM = pltpu.MemorySpace.VMEM
SMEM = pltpu.MemorySpace.SMEM
HBM = pltpu.MemorySpace.HBM


def place(dims):
    a_n, b_n, g_n, c_n = dims
    s, h = lax.axis_index("seq"), lax.axis_index("heads")
    return s // b_n, lax.rem(s, b_n), h // c_n, lax.rem(h, c_n)


def other(x, k, n):
    return lax.rem(x + k, n)


def along(x, k, n):
    if n & (n - 1):
        return lax.rem(x + k, n)
    bit = 1
    while bit < n:
        x = x + bit * ((k // bit) % 2) * (1 - 2 * ((x // bit) % 2))
        bit *= 2
    return x


def looped(start, stop, fn, backwards=False):
    if stop - start <= 8:
        for k in reversed(range(start, stop)) if backwards else range(start, stop):
            fn(k)
    else:
        lax.fori_loop(start, stop, lambda k, _: (fn(k), 0)[1], 0)


def hail(dims, me):
    a_n, b_n, g_n, c_n = dims
    a, b, g, c = me
    barrier = pltpu.get_barrier_semaphore()

    def signal(a2, b2, g2, c2):
        pl.semaphore_signal(
            barrier, inc=1, device_id=(g2 * c_n + c2, a2 * b_n + b2), device_id_type=MESH
        )

    for k in range(1, c_n):
        signal(a, b, g, other(c, k, c_n))
    for k in range(b_n):
        for n in range(g_n):
            if k or n:
                signal(a, other(b, k, b_n), other(g, n, g_n), c)
    for k in range(1, a_n):
        signal(other(a, k, a_n), b, g, c)


def meet(dims):
    a_n, b_n, g_n, c_n = dims
    pl.semaphore_wait(pltpu.get_barrier_semaphore(), a_n + b_n * g_n + c_n - 3)


def gather(
    dims, meanwhile, own_ref, g_ref, q_ref, sel_ref, out_ref, g_out, q_out, near_ref, near,
    g_raw, g_in_sem, q_in_sem, own_sem, a_sem, b_sem, c_sem, recv_sem, near_sem,
):
    a_n, b_n, g_n, c_n = dims
    me = place(dims)
    a, b, g, c = me
    hail(dims, me)
    mine = pltpu.make_async_copy(own_ref.at[0], out_ref.at[a * b_n + b, g * c_n + c], own_sem)
    mine.start()
    staged = pltpu.make_async_copy(g_ref, g_raw, g_in_sem)
    staged.start()
    heads, _, tokens = q_ref.shape
    across = [
        pltpu.make_async_copy(
            q_ref.at[h], q_out.at[:, h * tokens : (h + 1) * tokens], q_in_sem.at[h]
        )
        for h in range(heads)
    ]
    for cp in across:
        cp.start()
    meet(dims)
    asked = [
        pltpu.make_async_remote_copy(
            src_ref=sel_ref,
            dst_ref=near_ref.at[n],
            send_sem=near_sem.at[0, n],
            recv_sem=near_sem.at[1, n],
            device_id=(g * c_n + c, a * b_n + other(b, n, b_n)),
            device_id_type=MESH,
        )
        for n in range(1, b_n)
    ]

    swap = b_n == g_n
    flip = lax.rem(c, 2) if swap else 0

    def spot(ka, kp, kq, kc):
        kb, kg = (flip * kp + (1 - flip) * kq, (1 - flip) * kp + flip * kq) if swap else (kq, kp)
        return along(a, ka, a_n), other(b, kb, b_n), other(g, kg, g_n), other(c, kc, c_n)

    p_n, q_n = g_n, b_n

    def copy(key, step, sem, own):
        a1, b1, g1, c1 = spot(*key)
        a2, b2, g2, c2 = spot(*step)
        slot = (a1 * b_n + b1, g1 * c_n + c1)
        return pltpu.make_async_remote_copy(
            src_ref=own_ref.at[0] if own else out_ref.at[slot],
            dst_ref=out_ref.at[slot],
            send_sem=sem,
            recv_sem=recv_sem.at[slot],
            device_id=(g2 * c_n + c2, a2 * b_n + b2),
            device_id_type=MESH,
        )

    def arrived(*key):
        copy(key, (0, 0, 0, 0), own_sem, False).wait_recv()

    def sends(ka, kp, kq, own=False):
        key = (ka, kp, kq, 0)
        out = []
        if isinstance(kp, int) and kp == 0 and isinstance(kq, int) and kq == 0:
            out += [
                copy(key, (0, m, n, 0), b_sem.at[ka, m, n], own)
                for m in range(p_n) for n in range(q_n) if m or n
            ]
        out += [
            copy(key, (0, 0, 0, n), c_sem.at[ka * p_n + kp, kq, n], own) for n in range(1, c_n)
        ]
        return out

    def firsts():
        return [copy((0, 0, 0, 0), (n, 0, 0, 0), a_sem.at[n], True) for n in range(1, a_n)]

    def over_a(fn):
        if a_n <= 8:
            for ka in range(1, a_n):
                fn(ka)
        elif a_n > 1:
            lax.fori_loop(1, a_n, lambda ka, _: (fn(ka), 0)[1], 0)

    def relay(ka, kp, kq):
        arrived(ka, kp, kq, 0)
        for cp in sends(ka, kp, kq):
            cp.start()

    for cp in firsts() + sends(0, 0, 0, True) + asked:
        cp.start()
    staged.wait()
    g_out[...] = jnp.swapaxes(g_raw[...], 0, 1)
    for kp in range(1, p_n):
        relay(0, kp, 0)
    for kq in range(1, q_n):
        relay(0, 0, kq)
    over_a(lambda ka: relay(ka, 0, 0))
    for kp in range(1, p_n):
        for kq in range(1, q_n):
            relay(0, kp, kq)

    def last(ka):
        for kp in range(p_n):
            for kq in range(q_n):
                for kc in range(1, c_n):
                    arrived(ka, kp, kq, kc)

    for cp in asked:
        cp.wait()
    for n in range(1, b_n):
        noted = pltpu.make_async_copy(near_ref.at[n], near.at[n], near_sem.at[0, 0])
        noted.start()
        noted.wait()
    for cp in across:
        cp.wait()
    mine.wait()
    last(0)
    meanwhile()
    over_a(lambda ka: [relay(ka, kp, 0) for kp in range(1, p_n)])
    over_a(lambda ka: [relay(ka, 0, kq) for kq in range(1, q_n)])
    over_a(lambda ka: [relay(ka, kp, kq) for kp in range(1, p_n) for kq in range(1, q_n)])
    over_a(last)

    def finish():
        def sent(ka):
            for kp in range(p_n):
                for kq in range(q_n):
                    for cp in sends(ka, kp, kq):
                        cp.wait_send()

        sent(0)
        over_a(sent)
        for cp in firsts():
            cp.wait_send()

    return finish


def lay_keys(dims, keys, start, all_ref, block_of, many, strip):
    a_n, b_n, g_n, c_n = dims
    g = lax.axis_index("heads") // c_n
    parts = all_ref.shape[2] // strip

    def lay(at, k, h):
        nonlocal start
        for c1 in range(c_n):
            keys[start : start + strip, :] = all_ref[
                at, other(g, k, g_n) * c_n + c1, h * strip : (h + 1) * strip, :
            ]
            start += strip

    blocks = [block_of(p) for p in range(many)]
    for h in range(parts):
        for at in blocks:
            for k in range(1, g_n):
                lay(at, k, h)
    for h in range(parts):
        for at in blocks:
            lay(at, 0, h)


def attend(
    dims, scale, width, finish, sel_ref, near_ref, all_ref, q_ref, g_ref, o_ref, dq_ref, out_ref,
    keys, own_scores, own_grad, keys_t, probs, grads, o_rows, sent, kept, sent_in, kept_in, g_out, g_in, sums, x_out, z_out, z_in,
    c_sem, g_sem, x_sem, z_sem, *x_in,
):
    a_n, b_n, g_n, c_n = dims
    me = place(dims)
    a, b, g, c = me
    chosen = sel_ref.shape[1]
    heads, tokens, value_width = g_ref.shape
    key_width, columns = q_ref.shape
    strips, _, strip, _ = kept.shape
    parts = strips // (chosen + 1)
    many = parts * chosen
    block = own_scores.shape[0]
    before = keys.shape[0] - block
    f32, bf16 = jnp.float32, jnp.bfloat16
    across = (((1,), (1,)), ((), ()))
    down = (((0,), (0,)), ((), ()))
    share = strip * c_n
    runs = [(n * chosen, (n + 1) * chosen) for n in range(parts)]
    own = (many, strips)

    def copy(src, dst, sems, there):
        a2, b2, g2, c2 = there
        return pltpu.make_async_remote_copy(
            src_ref=src,
            dst_ref=dst,
            send_sem=sems.at[0],
            recv_sem=sems.at[1],
            device_id=(g2 * c_n + c2, a2 * b_n + b2),
            device_id_type=MESH,
        )

    def to_c(n, k):
        c2 = other(c, k, c_n)
        first, last = (runs + runs + [own, own])[n]
        at = pl.ds(first, last - first)
        if n < parts or n == 2 * parts:
            src, dst = sent.at[at, :, c2], sent_in.at[k, at]
        else:
            src, dst = kept.at[at, c2], kept_in.at[k, at]
        return copy(src, dst, c_sem.at[n, k], (a, b, g, c2))

    def to_g(n, k):
        first, last = (runs + [own])[n]
        at = pl.ds(first, last - first)
        return copy(g_out.at[k, at], g_in.at[k, at], g_sem.at[n, k], (a, b, other(g, k, g_n), c))

    def to_x(n, k):
        src, dst = x_out.at[pl.ds(n * chosen, chosen)], x_in[n].at[k, pl.ds(1, chosen)]
        return copy(src, dst, x_sem.at[n, k], (a, other(b, k, b_n), g, c))

    def to_z(h, k):
        return copy(z_out.at[h, k], z_in.at[h, k], z_sem.at[h, k], (along(a, k, a_n), b, g, c))

    for h in range(parts):
        sums[h, 0] = jnp.zeros(sums.shape[2:], f32)
        for k in range(1, b_n):
            x_in[h][k, 0] = jnp.zeros(x_in[h].shape[2:], bf16)

    lay_keys(dims, keys, 0, all_ref, lambda p: sel_ref[0, p], chosen, strip)

    def rows_of(n):
        return g_ref[n // tokens : (n + width) // tokens].reshape(width, value_width)

    for n in range(0, columns, width):
        at = slice(n, n + width)
        scores = jnp.dot(keys[:before, :], q_ref[:, at], preferred_element_type=f32)
        near_scores = own_scores[:, at]
        top = jnp.maximum(
            jnp.max(scores, axis=0, keepdims=True), jnp.max(near_scores, axis=0, keepdims=True)
        )
        weights = jnp.exp((scores - top) * scale)
        near_weights = jnp.exp((near_scores - top) * scale)
        norm = 1.0 / (
            jnp.sum(weights, axis=0, keepdims=True) + jnp.sum(near_weights, axis=0, keepdims=True)
        )
        grad_prob = lax.dot_general(
            keys[:before, :value_width], rows_of(n), across, preferred_element_type=f32
        )
        near_grad = own_grad[:, at]
        delta = norm * (
            jnp.sum(weights * grad_prob, axis=0, keepdims=True)
            + jnp.sum(near_weights * near_grad, axis=0, keepdims=True)
        )
        probs[:before, at] = (weights * norm).astype(bf16)
        probs[before:, at] = (near_weights * norm).astype(bf16)
        grads[:before, at] = (weights * (norm * scale) * (grad_prob - delta)).astype(bf16)
        grads[before:, at] = (near_weights * (norm * scale) * (near_grad - delta)).astype(bf16)

    def contribution(at):
        total = lax.dot_general(grads[at, :], q_ref[...], across, preferred_element_type=f32)
        value = jnp.dot(
            probs[at, :], g_ref[...].reshape(columns, value_width), preferred_element_type=f32
        )
        total = jnp.concatenate([total[:, :value_width] + value, total[:, value_width:]], axis=1)
        return total.astype(bf16)

    def hand_over(n):
        for k in range(1, c_n):
            to_c(n, k).start()

    def contribute_sent(h):
        high = chosen * (g_n - 1) * share
        first, last = runs[h]
        sent[first:last] = contribution(slice(h * high, (h + 1) * high)).reshape(
            (chosen,) + sent.shape[1:]
        )
        hand_over(h)

    def contribute_kept(h):
        first, last = runs[h]
        base = before - many * share
        kept[first:last] = contribution(slice(base + first * share, base + last * share)).reshape(
            (chosen,) + kept.shape[1:]
        )
        hand_over(parts + h)

    def contribute_own():
        total = contribution(slice(before, before + block))
        split = parts * (g_n - 1) * share
        sent[many:] = total[:split].reshape((parts,) + sent.shape[1:])
        kept[many:] = total[split:].reshape((parts,) + kept.shape[1:])
        hand_over(2 * parts)
        hand_over(2 * parts + 1)

    def take_over(n):
        for k in range(1, c_n):
            to_c(n, k).wait_recv()

    def to_groups(n):
        take_over(n if n < parts else 2 * parts)
        for m in range(1, g_n):
            for u in range(*(runs + [own])[n]):
                total = sent[u, m - 1, c].astype(f32)
                for k in range(1, c_n):
                    total += sent_in[k, u, m - 1].astype(f32)
                g_out[m, u] = total.astype(bf16)
            to_g(n, m).start()

    def from_groups(n):
        take_over(parts + n if n < parts else 2 * parts + 1)
        for k in range(1, g_n):
            to_g(n, k).wait_recv()

    def head_sum(u):
        total = kept[u, c].astype(f32)
        for k in range(1, c_n):
            total += kept_in[k, u].astype(f32)
        for k in range(1, g_n):
            total += g_in[k, u].astype(f32)
        return total

    def to_row(n):
        from_groups(n)
        for u in range(*runs[n]):
            total = head_sum(u)
            sums[n, u % chosen + 1] = total
            x_out[u] = total.astype(bf16)
        for k in range(1, b_n):
            to_x(n, k).start()

    def outputs(n):
        o_rows[n : n + width, :] = lax.dot_general(
            probs[:, n : n + width], keys[:, :value_width], down, preferred_element_type=f32
        ).astype(bf16)
        dq = jnp.dot(keys_t[...], grads[:, n : n + width], preferred_element_type=f32).astype(bf16)
        for m in range(width // tokens):
            dq_ref[n // tokens + m] = dq[:, m * tokens : (m + 1) * tokens]

    def slot(row, wanted):
        at = 0
        for p in range(chosen):
            at = jnp.where(row(p) == wanted, p + 1, at)
        return at

    def dense(h, a1):
        wanted = a1 * b_n + b
        total = sums[h, slot(lambda p: sel_ref[0, p], wanted)]
        for k in range(1, b_n):
            total += x_in[h][k, slot(lambda p: near_ref[k, 0, p], wanted)].astype(f32)
        return total

    def to_holders(h):
        for k in range(1, b_n):
            to_x(h, k).wait_recv()

        def send(k):
            z_out[h, k] = dense(h, along(a, k, a_n)).astype(bf16)
            to_z(h, k).start()

        looped(1, a_n, send, True)
        out_ref[h * strip : (h + 1) * strip, :] = dense(h, a)

    starts = list(range(0, columns, width))
    cuts = [len(starts) * n // (parts + 2) for n in range(parts + 3)]

    def some_outputs(n):
        for m in starts[cuts[n] : cuts[n + 1]]:
            outputs(m)

    for n in range(parts):
        contribute_sent(n)
    to_groups(0)
    for n in range(parts):
        contribute_kept(n)
        if n + 1 < parts:
            to_groups(n + 1)
    keys_t[...] = keys[...].T
    to_row(0)
    contribute_own()
    for n in range(1, parts):
        to_row(n)
    to_groups(parts)
    for n in range(parts):
        to_holders(n)
        if n == 0:
            some_outputs(0)
    some_outputs(1)
    some_outputs(2)
    some_outputs(parts + 1)
    part = 8 if heads % 8 == 0 else heads
    for h in range(0, heads, part):
        o_ref[:, h : h + part, :] = jnp.swapaxes(
            o_rows[h * tokens : (h + part) * tokens, :].reshape(part, tokens, value_width), 0, 1
        )
    from_groups(parts)
    for h in range(parts):
        out_ref[h * strip : (h + 1) * strip, :] += head_sum(many + h)
    finish()
    for n in range(2 * parts + 2):
        for k in range(1, c_n):
            to_c(n, k).wait_send()
    for n in range(parts + 1):
        for k in range(1, g_n):
            to_g(n, k).wait_send()
        if n < parts:
            for k in range(1, b_n):
                to_x(n, k).wait_send()
    for h in range(parts):
        looped(1, a_n, lambda k: to_z(h, k).wait_send())

        def take(k):
            to_z(h, k).wait_recv()
            out_ref[h * strip : (h + 1) * strip, :] += z_in[h, k].astype(f32)

        looped(1, a_n, take)


def layer_kernel(
    dims, scale, width, sel_ref, sel_raw, own_ref, q_raw, g_in, o_ref, dq_ref, out_ref,
    pieces, g_rows, q_cols, near_raw, near, *refs,
):
    keys, own_scores, own_grad = refs[9:12]
    block = own_scores.shape[0]
    before = keys.shape[0] - block
    tokens, value_width = g_rows.shape[1:]

    def own_block():
        at = lax.axis_index("seq")
        lay_keys(dims, keys, before, pieces, lambda p: at, 1, refs[17].shape[2])
        for n in range(0, q_cols.shape[1], width):
            rows = g_rows[n // tokens : (n + width) // tokens].reshape(width, value_width)
            own_scores[:, n : n + width] = jnp.dot(
                keys[before:, :], q_cols[:, n : n + width], preferred_element_type=jnp.float32
            )
            own_grad[:, n : n + width] = lax.dot_general(
                keys[before:, :value_width], rows, (((1,), (1,)), ((), ())),
                preferred_element_type=jnp.float32,
            )

    finish = gather(
        dims, own_block, own_ref, g_in, q_raw, sel_raw, pieces, g_rows, q_cols, near_raw, near,
        *refs[:9],
    )
    attend(
        dims, scale, width, finish, sel_ref, near, pieces, q_cols, g_rows, o_ref, dq_ref, out_ref,
        *refs[9:],
    )


def layer(selected, latents, queries, grad_out, dims):
    a_n, b_n, g_n, c_n = dims
    n_s, n_h = a_n * b_n, g_n * c_n
    heads, key_width, tokens = queries.shape
    value_width = grad_out.shape[2]
    columns = heads * tokens
    count = selected.shape[1] + 1
    rows = latents.shape[1]
    keys = count * rows * n_h
    one = (rows, key_width)
    parts = 2 if rows % 32 == 0 else 1
    strips = parts * count
    strip = (rows // parts, key_width)
    dma = pltpu.SemaphoreType.DMA
    half = functools.partial(pltpu.VMEM, dtype=jnp.bfloat16)
    width = tokens * (4 if heads % 4 == 0 else 1)
    return pl.pallas_call(
        functools.partial(layer_kernel, dims, key_width ** (-0.5), width),
        out_shape=(
            half((tokens, heads, value_width)),
            half((heads, key_width, tokens)),
            pltpu.VMEM(one, jnp.float32),
        ),
        in_specs=[pl.BlockSpec(memory_space=SMEM)] + [pl.BlockSpec(memory_space=HBM)] * 4,
        out_specs=[pl.BlockSpec(memory_space=VMEM)] * 3,
        scratch_shapes=[
            half((n_s, n_h) + one),
            half((heads, tokens, value_width)),
            half((key_width, columns)),
            pltpu.VMEM((b_n,) + selected.shape, selected.dtype),
            SMEM((b_n,) + selected.shape, selected.dtype),
            half(grad_out.shape),
            dma,
            dma((heads,)),
            dma,
            dma((a_n,)),
            dma((a_n, g_n, b_n)),
            dma((a_n * g_n, b_n, c_n)),
            dma((n_s, n_h)),
            dma((2, b_n)),
            half((keys, key_width)),
            pltpu.VMEM((rows * n_h, columns), jnp.float32),
            pltpu.VMEM((rows * n_h, columns), jnp.float32),
            half((key_width, keys)),
            half((keys, columns)),
            half((keys, columns)),
            half((columns, value_width)),
            half((strips, g_n - 1, c_n) + strip),
            half((strips, c_n) + strip),
            half((c_n, strips, g_n - 1) + strip),
            half((c_n, strips) + strip),
            half((g_n, strips) + strip),
            half((g_n, strips) + strip),
            pltpu.VMEM((parts, count) + strip, jnp.float32),
            half((strips,) + strip),
            half((parts, a_n) + strip),
            half((parts, a_n) + strip),
            dma((2 * parts + 2, c_n, 2)),
            dma((parts + 1, g_n, 2)),
            dma((parts, b_n, 2)),
            dma((parts, a_n, 2)),
        ] + [half((b_n, count) + strip)] * parts,
        compiler_params=pltpu.CompilerParams(
            collective_id=0, has_side_effects=True, vmem_limit_bytes=67043328 - 5500000
        ),
        name="layer",
    )(selected, selected, latents, queries, grad_out)


def hand_out_kernel(*refs):
    n = (len(refs) - 1) // 2
    copies = [pltpu.make_async_copy(refs[k], refs[n + k], refs[-1].at[k]) for k in range(n)]
    for cp in copies:
        cp.start()
    for cp in copies:
        cp.wait()


def hand_out(arrays):
    return pl.pallas_call(
        hand_out_kernel,
        out_shape=[jax.ShapeDtypeStruct(x.shape, x.dtype) for x in arrays],
        in_specs=[pl.BlockSpec(memory_space=VMEM) for _ in arrays],
        out_specs=[pl.BlockSpec(memory_space=HBM) for _ in arrays],
        scratch_shapes=[pltpu.SemaphoreType.DMA((len(arrays),))],
        compiler_params=pltpu.CompilerParams(vmem_limit_bytes=16 * 1024 * 1024),
        name="hand_out",
    )(*arrays)


def shards(dims, queries, latents, grad_out, selected):
    assert latents.shape[0] == 1
    output, grad_query, latent_grad = hand_out(
        layer(selected, latents, jnp.transpose(queries, (1, 2, 0)), grad_out, dims)
    )
    return output, jnp.transpose(grad_query, (2, 0, 1)), latent_grad[None]


def solution(mesh):
    n_h, n_s = mesh.shape["heads"], mesh.shape["seq"]
    b_n = 2 if n_s % 2 == 0 else 1
    c_n = 2 if n_h % 2 == 0 else 1
    dims = (n_s // b_n, b_n, n_h // c_n, c_n)
    in_specs = (
        P("seq", "heads", None),
        P("seq", "heads", None),
        P("seq", "heads", None),
        P("seq", None),
    )
    out_specs = (P("seq", "heads", None), P("seq", "heads", None), P("seq", "heads", None))
    return jax.shard_map(
        functools.partial(shards, dims),
        mesh=mesh, in_specs=in_specs, out_specs=out_specs, check_vma=False,
    )
```

```python
import functools

import jax
import jax.numpy as jnp
from jax import lax
from jax.experimental import pallas as pl
from jax.experimental.pallas import tpu as pltpu
from jax.sharding import PartitionSpec as P

MESH = pl.DeviceIdType.MESH
VMEM = pltpu.MemorySpace.VMEM
SMEM = pltpu.MemorySpace.SMEM
HBM = pltpu.MemorySpace.HBM


def place(dims):
    a_n, b_n, g_n, c_n = dims
    s, h = lax.axis_index("seq"), lax.axis_index("heads")
    return s // b_n, lax.rem(s, b_n), h // c_n, lax.rem(h, c_n)


def other(x, k, n):
    return lax.rem(x + k, n)


def along(x, k, n):
    if n & (n - 1):
        return lax.rem(x + k, n)
    bit = 1
    while bit < n:
        x = x + bit * ((k // bit) % 2) * (1 - 2 * ((x // bit) % 2))
        bit *= 2
    return x


def looped(start, stop, fn, backwards=False):
    if stop - start <= 8:
        for k in reversed(range(start, stop)) if backwards else range(start, stop):
            fn(k)
    else:
        lax.fori_loop(start, stop, lambda k, _: (fn(k), 0)[1], 0)


def hail(dims, me):
    a_n, b_n, g_n, c_n = dims
    a, b, g, c = me
    barrier = pltpu.get_barrier_semaphore()

    def signal(a2, b2, g2, c2):
        pl.semaphore_signal(
            barrier, inc=1, device_id=(g2 * c_n + c2, a2 * b_n + b2), device_id_type=MESH
        )

    for k in range(1, c_n):
        signal(a, b, g, other(c, k, c_n))
    for k in range(b_n):
        for n in range(g_n):
            if k or n:
                signal(a, other(b, k, b_n), other(g, n, g_n), c)
    for k in range(1, a_n):
        signal(other(a, k, a_n), b, g, c)


def meet(dims):
    a_n, b_n, g_n, c_n = dims
    pl.semaphore_wait(pltpu.get_barrier_semaphore(), a_n + b_n * g_n + c_n - 3)


def gather(
    dims, meanwhile, own_ref, g_ref, q_ref, sel_ref, out_ref, g_out, q_out, near_ref, near,
    g_raw, g_in_sem, q_in_sem, own_sem, a_sem, b_sem, c_sem, recv_sem, near_sem,
):
    a_n, b_n, g_n, c_n = dims
    me = place(dims)
    a, b, g, c = me
    hail(dims, me)
    mine = pltpu.make_async_copy(own_ref.at[0], out_ref.at[a * b_n + b, g * c_n + c], own_sem)
    mine.start()
    noted = pltpu.make_async_copy(sel_ref, near.at[0], near_sem.at[0, 0])
    noted.start()
    staged = pltpu.make_async_copy(g_ref, g_raw, g_in_sem)
    staged.start()
    heads, _, tokens = q_ref.shape
    across = [
        pltpu.make_async_copy(
            q_ref.at[h], q_out.at[:, h * tokens : (h + 1) * tokens], q_in_sem.at[h]
        )
        for h in range(heads)
    ]
    for cp in across:
        cp.start()
    meet(dims)
    asked = [
        pltpu.make_async_remote_copy(
            src_ref=sel_ref,
            dst_ref=near_ref.at[n],
            send_sem=near_sem.at[0, n],
            recv_sem=near_sem.at[1, n],
            device_id=(g * c_n + c, a * b_n + other(b, n, b_n)),
            device_id_type=MESH,
        )
        for n in range(1, b_n)
    ]

    swap = b_n == g_n
    flip = lax.rem(c, 2) if swap else 0

    def spot(ka, kp, kq, kc):
        kb, kg = (flip * kp + (1 - flip) * kq, (1 - flip) * kp + flip * kq) if swap else (kq, kp)
        return along(a, ka, a_n), other(b, kb, b_n), other(g, kg, g_n), other(c, kc, c_n)

    p_n, q_n = g_n, b_n

    def copy(key, step, sem, own):
        a1, b1, g1, c1 = spot(*key)
        a2, b2, g2, c2 = spot(*step)
        slot = (a1 * b_n + b1, g1 * c_n + c1)
        return pltpu.make_async_remote_copy(
            src_ref=own_ref.at[0] if own else out_ref.at[slot],
            dst_ref=out_ref.at[slot],
            send_sem=sem,
            recv_sem=recv_sem.at[slot],
            device_id=(g2 * c_n + c2, a2 * b_n + b2),
            device_id_type=MESH,
        )

    def arrived(*key):
        copy(key, (0, 0, 0, 0), own_sem, False).wait_recv()

    def sends(ka, kp, kq, own=False):
        key = (ka, kp, kq, 0)
        out = []
        if isinstance(kp, int) and kp == 0 and isinstance(kq, int) and kq == 0:
            out += [
                copy(key, (0, m, n, 0), b_sem.at[ka, m, n], own)
                for m in range(p_n) for n in range(q_n) if m or n
            ]
        out += [
            copy(key, (0, 0, 0, n), c_sem.at[ka * p_n + kp, kq, n], own) for n in range(1, c_n)
        ]
        return out

    def firsts():
        return [copy((0, 0, 0, 0), (n, 0, 0, 0), a_sem.at[n], True) for n in range(1, a_n)]

    def over_a(fn):
        if a_n <= 8:
            for ka in range(1, a_n):
                fn(ka)
        elif a_n > 1:
            lax.fori_loop(1, a_n, lambda ka, _: (fn(ka), 0)[1], 0)

    def relay(ka, kp, kq):
        arrived(ka, kp, kq, 0)
        for cp in sends(ka, kp, kq):
            cp.start()

    for cp in firsts() + sends(0, 0, 0, True) + asked:
        cp.start()
    staged.wait()
    g_out[...] = jnp.swapaxes(g_raw[...], 0, 1)
    for kp in range(1, p_n):
        relay(0, kp, 0)
    for kq in range(1, q_n):
        relay(0, 0, kq)
    over_a(lambda ka: relay(ka, 0, 0))
    for kp in range(1, p_n):
        for kq in range(1, q_n):
            relay(0, kp, kq)

    def last(ka):
        for kp in range(p_n):
            for kq in range(q_n):
                for kc in range(1, c_n):
                    arrived(ka, kp, kq, kc)

    for cp in asked:
        cp.wait()
    noted.wait()
    for n in range(1, b_n):
        noted = pltpu.make_async_copy(near_ref.at[n], near.at[n], near_sem.at[0, 0])
        noted.start()
        noted.wait()
    for cp in across:
        cp.wait()
    mine.wait()
    last(0)
    meanwhile()
    over_a(lambda ka: [relay(ka, kp, 0) for kp in range(1, p_n)])
    over_a(lambda ka: [relay(ka, 0, kq) for kq in range(1, q_n)])
    over_a(lambda ka: [relay(ka, kp, kq) for kp in range(1, p_n) for kq in range(1, q_n)])
    over_a(last)

    def finish():
        def sent(ka):
            for kp in range(p_n):
                for kq in range(q_n):
                    for cp in sends(ka, kp, kq):
                        cp.wait_send()

        sent(0)
        over_a(sent)
        for cp in firsts():
            cp.wait_send()

    return finish


def lay_keys(dims, keys, start, all_ref, block_of, many, strip):
    a_n, b_n, g_n, c_n = dims
    g = lax.axis_index("heads") // c_n
    parts = all_ref.shape[2] // strip

    def lay(at, k, h):
        nonlocal start
        for c1 in range(c_n):
            keys[start : start + strip, :] = all_ref[
                at, other(g, k, g_n) * c_n + c1, h * strip : (h + 1) * strip, :
            ]
            start += strip

    blocks = [block_of(p) for p in range(many)]
    for h in range(parts):
        for at in blocks:
            for k in range(1, g_n):
                lay(at, k, h)
    for h in range(parts):
        for at in blocks:
            lay(at, 0, h)


def attend(
    dims, scale, width, finish, near_ref, all_ref, q_ref, g_ref, o_ref, dq_ref, out_ref,
    keys, own_scores, own_grad, keys_t, probs, grads, o_rows, sent, kept, sent_in, kept_in, g_out, g_in, sums, x_out, z_out, z_in,
    c_sem, g_sem, x_sem, z_sem, *x_in,
):
    a_n, b_n, g_n, c_n = dims
    me = place(dims)
    a, b, g, c = me
    chosen = near_ref.shape[2]
    heads, tokens, value_width = g_ref.shape
    key_width, columns = q_ref.shape
    strips, _, strip, _ = kept.shape
    parts = strips // (chosen + 1)
    many = parts * chosen
    block = own_scores.shape[0]
    before = keys.shape[0] - block
    f32, bf16 = jnp.float32, jnp.bfloat16
    across = (((1,), (1,)), ((), ()))
    down = (((0,), (0,)), ((), ()))
    share = strip * c_n
    runs = [(n * chosen, (n + 1) * chosen) for n in range(parts)]
    own = (many, strips)

    def copy(src, dst, sems, there):
        a2, b2, g2, c2 = there
        return pltpu.make_async_remote_copy(
            src_ref=src,
            dst_ref=dst,
            send_sem=sems.at[0],
            recv_sem=sems.at[1],
            device_id=(g2 * c_n + c2, a2 * b_n + b2),
            device_id_type=MESH,
        )

    def to_c(n, k):
        c2 = other(c, k, c_n)
        first, last = (runs + runs + [own, own])[n]
        at = pl.ds(first, last - first)
        if n < parts or n == 2 * parts:
            src, dst = sent.at[at, :, c2], sent_in.at[k, at]
        else:
            src, dst = kept.at[at, c2], kept_in.at[k, at]
        return copy(src, dst, c_sem.at[n, k], (a, b, g, c2))

    def to_g(n, k):
        first, last = (runs + [own])[n]
        at = pl.ds(first, last - first)
        return copy(g_out.at[k, at], g_in.at[k, at], g_sem.at[n, k], (a, b, other(g, k, g_n), c))

    def to_x(n, k):
        src, dst = x_out.at[pl.ds(n * chosen, chosen)], x_in[n].at[k, pl.ds(1, chosen)]
        return copy(src, dst, x_sem.at[n, k], (a, other(b, k, b_n), g, c))

    def to_z(h, k):
        return copy(z_out.at[h, k], z_in.at[h, k], z_sem.at[h, k], (along(a, k, a_n), b, g, c))

    for h in range(parts):
        sums[h, 0] = jnp.zeros(sums.shape[2:], f32)
        for k in range(1, b_n):
            x_in[h][k, 0] = jnp.zeros(x_in[h].shape[2:], bf16)

    lay_keys(dims, keys, 0, all_ref, lambda p: near_ref[0, 0, p], chosen, strip)

    def rows_of(n):
        return g_ref[n // tokens : (n + width) // tokens].reshape(width, value_width)

    for n in range(0, columns, width):
        at = slice(n, n + width)
        scores = jnp.dot(keys[:before, :], q_ref[:, at], preferred_element_type=f32)
        near_scores = own_scores[:, at]
        top = jnp.maximum(
            jnp.max(scores, axis=0, keepdims=True), jnp.max(near_scores, axis=0, keepdims=True)
        )
        weights = jnp.exp((scores - top) * scale)
        near_weights = jnp.exp((near_scores - top) * scale)
        norm = 1.0 / (
            jnp.sum(weights, axis=0, keepdims=True) + jnp.sum(near_weights, axis=0, keepdims=True)
        )
        grad_prob = lax.dot_general(
            keys[:before, :value_width], rows_of(n), across, preferred_element_type=f32
        )
        near_grad = own_grad[:, at]
        delta = norm * (
            jnp.sum(weights * grad_prob, axis=0, keepdims=True)
            + jnp.sum(near_weights * near_grad, axis=0, keepdims=True)
        )
        probs[:before, at] = (weights * norm).astype(bf16)
        probs[before:, at] = (near_weights * norm).astype(bf16)
        grads[:before, at] = (weights * (norm * scale) * (grad_prob - delta)).astype(bf16)
        grads[before:, at] = (near_weights * (norm * scale) * (near_grad - delta)).astype(bf16)

    def contribution(at):
        total = lax.dot_general(grads[at, :], q_ref[...], across, preferred_element_type=f32)
        value = jnp.dot(
            probs[at, :], g_ref[...].reshape(columns, value_width), preferred_element_type=f32
        )
        total = jnp.concatenate([total[:, :value_width] + value, total[:, value_width:]], axis=1)
        return total.astype(bf16)

    def hand_over(n):
        for k in range(1, c_n):
            to_c(n, k).start()

    def contribute_sent(h):
        high = chosen * (g_n - 1) * share
        first, last = runs[h]
        sent[first:last] = contribution(slice(h * high, (h + 1) * high)).reshape(
            (chosen,) + sent.shape[1:]
        )
        hand_over(h)

    def contribute_kept(h):
        first, last = runs[h]
        base = before - many * share
        kept[first:last] = contribution(slice(base + first * share, base + last * share)).reshape(
            (chosen,) + kept.shape[1:]
        )
        hand_over(parts + h)

    def contribute_own():
        total = contribution(slice(before, before + block))
        split = parts * (g_n - 1) * share
        sent[many:] = total[:split].reshape((parts,) + sent.shape[1:])
        kept[many:] = total[split:].reshape((parts,) + kept.shape[1:])
        hand_over(2 * parts)
        hand_over(2 * parts + 1)

    def take_over(n):
        for k in range(1, c_n):
            to_c(n, k).wait_recv()

    def to_groups(n):
        take_over(n if n < parts else 2 * parts)
        for m in range(1, g_n):
            for u in range(*(runs + [own])[n]):
                total = sent[u, m - 1, c].astype(f32)
                for k in range(1, c_n):
                    total += sent_in[k, u, m - 1].astype(f32)
                g_out[m, u] = total.astype(bf16)
            to_g(n, m).start()

    def from_groups(n):
        take_over(parts + n if n < parts else 2 * parts + 1)
        for k in range(1, g_n):
            to_g(n, k).wait_recv()

    def head_sum(u):
        total = kept[u, c].astype(f32)
        for k in range(1, c_n):
            total += kept_in[k, u].astype(f32)
        for k in range(1, g_n):
            total += g_in[k, u].astype(f32)
        return total

    def to_row(n):
        from_groups(n)
        for u in range(*runs[n]):
            total = head_sum(u)
            sums[n, u % chosen + 1] = total
            x_out[u] = total.astype(bf16)
        for k in range(1, b_n):
            to_x(n, k).start()

    def outputs(n):
        o_rows[n : n + width, :] = lax.dot_general(
            probs[:, n : n + width], keys[:, :value_width], down, preferred_element_type=f32
        ).astype(bf16)
        dq = jnp.dot(keys_t[...], grads[:, n : n + width], preferred_element_type=f32).astype(bf16)
        for m in range(width // tokens):
            dq_ref[n // tokens + m] = dq[:, m * tokens : (m + 1) * tokens]

    def slot(row, wanted):
        at = 0
        for p in range(chosen):
            at = jnp.where(row(p) == wanted, p + 1, at)
        return at

    def dense(h, a1):
        wanted = a1 * b_n + b
        total = sums[h, slot(lambda p: near_ref[0, 0, p], wanted)]
        for k in range(1, b_n):
            total += x_in[h][k, slot(lambda p: near_ref[k, 0, p], wanted)].astype(f32)
        return total

    def to_holders(h):
        for k in range(1, b_n):
            to_x(h, k).wait_recv()

        def send(k):
            z_out[h, k] = dense(h, along(a, k, a_n)).astype(bf16)
            to_z(h, k).start()

        looped(1, a_n, send, True)
        out_ref[h * strip : (h + 1) * strip, :] = dense(h, a)

    starts = list(range(0, columns, width))
    cuts = [len(starts) * n // (parts + 2) for n in range(parts + 3)]

    def some_outputs(n):
        for m in starts[cuts[n] : cuts[n + 1]]:
            outputs(m)

    for n in range(parts):
        contribute_sent(n)
    to_groups(0)
    for n in range(parts):
        contribute_kept(n)
        if n + 1 < parts:
            to_groups(n + 1)
    keys_t[...] = keys[...].T
    to_row(0)
    contribute_own()
    for n in range(1, parts):
        to_row(n)
    to_groups(parts)
    for n in range(parts):
        to_holders(n)
        if n == 0:
            some_outputs(0)
    some_outputs(1)
    some_outputs(2)
    some_outputs(parts + 1)
    part = 8 if heads % 8 == 0 else heads
    for h in range(0, heads, part):
        o_ref[:, h : h + part, :] = jnp.swapaxes(
            o_rows[h * tokens : (h + part) * tokens, :].reshape(part, tokens, value_width), 0, 1
        )
    from_groups(parts)
    for h in range(parts):
        out_ref[h * strip : (h + 1) * strip, :] += head_sum(many + h)
    finish()
    for n in range(2 * parts + 2):
        for k in range(1, c_n):
            to_c(n, k).wait_send()
    for n in range(parts + 1):
        for k in range(1, g_n):
            to_g(n, k).wait_send()
        if n < parts:
            for k in range(1, b_n):
                to_x(n, k).wait_send()
    for h in range(parts):
        looped(1, a_n, lambda k: to_z(h, k).wait_send())

        def take(k):
            to_z(h, k).wait_recv()
            out_ref[h * strip : (h + 1) * strip, :] += z_in[h, k].astype(f32)

        looped(1, a_n, take)


def layer_kernel(
    dims, scale, width, sel_raw, own_ref, q_raw, g_in, o_ref, dq_ref, out_ref,
    pieces, g_rows, q_cols, near_raw, near, *refs,
):
    keys, own_scores, own_grad = refs[9:12]
    block = own_scores.shape[0]
    before = keys.shape[0] - block
    tokens, value_width = g_rows.shape[1:]

    def own_block():
        at = lax.axis_index("seq")
        lay_keys(dims, keys, before, pieces, lambda p: at, 1, refs[17].shape[2])
        for n in range(0, q_cols.shape[1], width):
            rows = g_rows[n // tokens : (n + width) // tokens].reshape(width, value_width)
            own_scores[:, n : n + width] = jnp.dot(
                keys[before:, :], q_cols[:, n : n + width], preferred_element_type=jnp.float32
            )
            own_grad[:, n : n + width] = lax.dot_general(
                keys[before:, :value_width], rows, (((1,), (1,)), ((), ())),
                preferred_element_type=jnp.float32,
            )

    finish = gather(
        dims, own_block, own_ref, g_in, q_raw, sel_raw, pieces, g_rows, q_cols, near_raw, near,
        *refs[:9],
    )
    attend(
        dims, scale, width, finish, near, pieces, q_cols, g_rows, o_ref, dq_ref, out_ref,
        *refs[9:],
    )


def layer(selected, latents, queries, grad_out, dims):
    a_n, b_n, g_n, c_n = dims
    n_s, n_h = a_n * b_n, g_n * c_n
    heads, key_width, tokens = queries.shape
    value_width = grad_out.shape[2]
    columns = heads * tokens
    count = selected.shape[1] + 1
    rows = latents.shape[1]
    keys = count * rows * n_h
    one = (rows, key_width)
    parts = 2 if rows % 32 == 0 else 1
    strips = parts * count
    strip = (rows // parts, key_width)
    dma = pltpu.SemaphoreType.DMA
    half = functools.partial(pltpu.VMEM, dtype=jnp.bfloat16)
    width = tokens * (4 if heads % 4 == 0 else 1)
    return pl.pallas_call(
        functools.partial(layer_kernel, dims, key_width ** (-0.5), width),
        out_shape=(
            half((tokens, heads, value_width)),
            half((heads, key_width, tokens)),
            pltpu.VMEM(one, jnp.float32),
        ),
        in_specs=[pl.BlockSpec(memory_space=HBM)] * 4,
        out_specs=[pl.BlockSpec(memory_space=VMEM)] * 3,
        scratch_shapes=[
            half((n_s, n_h) + one),
            half((heads, tokens, value_width)),
            half((key_width, columns)),
            pltpu.VMEM((b_n,) + selected.shape, selected.dtype),
            SMEM((b_n,) + selected.shape, selected.dtype),
            half(grad_out.shape),
            dma,
            dma((heads,)),
            dma,
            dma((a_n,)),
            dma((a_n, g_n, b_n)),
            dma((a_n * g_n, b_n, c_n)),
            dma((n_s, n_h)),
            dma((2, b_n)),
            half((keys, key_width)),
            pltpu.VMEM((rows * n_h, columns), jnp.float32),
            pltpu.VMEM((rows * n_h, columns), jnp.float32),
            half((key_width, keys)),
            half((keys, columns)),
            half((keys, columns)),
            half((columns, value_width)),
            half((strips, g_n - 1, c_n) + strip),
            half((strips, c_n) + strip),
            half((c_n, strips, g_n - 1) + strip),
            half((c_n, strips) + strip),
            half((g_n, strips) + strip),
            half((g_n, strips) + strip),
            pltpu.VMEM((parts, count) + strip, jnp.float32),
            half((strips,) + strip),
            half((parts, a_n) + strip),
            half((parts, a_n) + strip),
            dma((2 * parts + 2, c_n, 2)),
            dma((parts + 1, g_n, 2)),
            dma((parts, b_n, 2)),
            dma((parts, a_n, 2)),
        ] + [half((b_n, count) + strip)] * parts,
        compiler_params=pltpu.CompilerParams(
            collective_id=0, has_side_effects=True, vmem_limit_bytes=67043328 - 5500000
        ),
        name="layer",
    )(selected, latents, queries, grad_out)


def hand_out_kernel(*refs):
    n = (len(refs) - 1) // 2
    copies = [pltpu.make_async_copy(refs[k], refs[n + k], refs[-1].at[k]) for k in range(n)]
    for cp in copies:
        cp.start()
    for cp in copies:
        cp.wait()


def hand_out(arrays):
    return pl.pallas_call(
        hand_out_kernel,
        out_shape=[jax.ShapeDtypeStruct(x.shape, x.dtype) for x in arrays],
        in_specs=[pl.BlockSpec(memory_space=VMEM) for _ in arrays],
        out_specs=[pl.BlockSpec(memory_space=HBM) for _ in arrays],
        scratch_shapes=[pltpu.SemaphoreType.DMA((len(arrays),))],
        compiler_params=pltpu.CompilerParams(vmem_limit_bytes=16 * 1024 * 1024),
        name="hand_out",
    )(*arrays)


def shards(dims, queries, latents, grad_out, selected):
    assert latents.shape[0] == 1
    output, grad_query, latent_grad = hand_out(
        layer(selected, latents, jnp.transpose(queries, (1, 2, 0)), grad_out, dims)
    )
    return output, jnp.transpose(grad_query, (2, 0, 1)), latent_grad[None]


def solution(mesh):
    n_h, n_s = mesh.shape["heads"], mesh.shape["seq"]
    b_n = 2 if n_s % 2 == 0 else 1
    c_n = 2 if n_h % 2 == 0 else 1
    dims = (n_s // b_n, b_n, n_h // c_n, c_n)
    in_specs = (
        P("seq", "heads", None),
        P("seq", "heads", None),
        P("seq", "heads", None),
        P("seq", None),
    )
    out_specs = (P("seq", "heads", None), P("seq", "heads", None), P("seq", "heads", None))
    return jax.shard_map(
        functools.partial(shards, dims),
        mesh=mesh, in_specs=in_specs, out_specs=out_specs, check_vma=False,
    )
```

```python
import functools

import jax
import jax.numpy as jnp
from jax import lax
from jax.experimental import pallas as pl
from jax.experimental.pallas import tpu as pltpu
from jax.sharding import PartitionSpec as P

MESH = pl.DeviceIdType.MESH
VMEM = pltpu.MemorySpace.VMEM
SMEM = pltpu.MemorySpace.SMEM
HBM = pltpu.MemorySpace.HBM


def place(dims):
    a_n, b_n, g_n, c_n = dims
    s, h = lax.axis_index("seq"), lax.axis_index("heads")
    return s // b_n, lax.rem(s, b_n), h // c_n, lax.rem(h, c_n)


def other(x, k, n):
    return lax.rem(x + k, n)


def along(x, k, n):
    if n & (n - 1):
        return lax.rem(x + k, n)
    bit = 1
    while bit < n:
        x = x + bit * ((k // bit) % 2) * (1 - 2 * ((x // bit) % 2))
        bit *= 2
    return x


def looped(start, stop, fn, backwards=False):
    if stop - start <= 8:
        for k in reversed(range(start, stop)) if backwards else range(start, stop):
            fn(k)
    else:
        lax.fori_loop(start, stop, lambda k, _: (fn(k), 0)[1], 0)


def hail(dims, me):
    a_n, b_n, g_n, c_n = dims
    a, b, g, c = me
    barrier = pltpu.get_barrier_semaphore()

    def signal(a2, b2, g2, c2):
        pl.semaphore_signal(
            barrier, inc=1, device_id=(g2 * c_n + c2, a2 * b_n + b2), device_id_type=MESH
        )

    for k in range(1, a_n):
        signal(other(a, k, a_n), b, g, c)
    for k in range(1, c_n):
        signal(a, b, g, other(c, k, c_n))
    for k in range(b_n):
        for n in range(g_n):
            if k or n:
                signal(a, other(b, k, b_n), other(g, n, g_n), c)


def meet(dims):
    a_n, b_n, g_n, c_n = dims
    pl.semaphore_wait(pltpu.get_barrier_semaphore(), a_n + b_n * g_n + c_n - 3)


def gather(
    dims, meanwhile, own_ref, g_ref, q_ref, sel_ref, out_ref, g_out, q_out, near_ref, near,
    g_raw, g_in_sem, q_in_sem, own_sem, a_sem, b_sem, c_sem, recv_sem, near_sem,
):
    a_n, b_n, g_n, c_n = dims
    me = place(dims)
    a, b, g, c = me
    hail(dims, me)
    mine = pltpu.make_async_copy(own_ref.at[0], out_ref.at[a * b_n + b, g * c_n + c], own_sem)
    mine.start()
    noted = pltpu.make_async_copy(sel_ref, near.at[0], near_sem.at[0, 0])
    noted.start()
    staged = pltpu.make_async_copy(g_ref, g_raw, g_in_sem)
    staged.start()
    heads, _, tokens = q_ref.shape
    across = [
        pltpu.make_async_copy(
            q_ref.at[h], q_out.at[:, h * tokens : (h + 1) * tokens], q_in_sem.at[h]
        )
        for h in range(heads)
    ]
    for cp in across:
        cp.start()
    meet(dims)
    asked = [
        pltpu.make_async_remote_copy(
            src_ref=sel_ref,
            dst_ref=near_ref.at[n],
            send_sem=near_sem.at[0, n],
            recv_sem=near_sem.at[1, n],
            device_id=(g * c_n + c, a * b_n + other(b, n, b_n)),
            device_id_type=MESH,
        )
        for n in range(1, b_n)
    ]

    swap = b_n == g_n
    flip = lax.rem(c, 2) if swap else 0

    def spot(ka, kp, kq, kc):
        kb, kg = (flip * kp + (1 - flip) * kq, (1 - flip) * kp + flip * kq) if swap else (kq, kp)
        return along(a, ka, a_n), other(b, kb, b_n), other(g, kg, g_n), other(c, kc, c_n)

    p_n, q_n = g_n, b_n

    def copy(key, step, sem, own):
        a1, b1, g1, c1 = spot(*key)
        a2, b2, g2, c2 = spot(*step)
        slot = (a1 * b_n + b1, g1 * c_n + c1)
        return pltpu.make_async_remote_copy(
            src_ref=own_ref.at[0] if own else out_ref.at[slot],
            dst_ref=out_ref.at[slot],
            send_sem=sem,
            recv_sem=recv_sem.at[slot],
            device_id=(g2 * c_n + c2, a2 * b_n + b2),
            device_id_type=MESH,
        )

    def arrived(*key):
        copy(key, (0, 0, 0, 0), own_sem, False).wait_recv()

    def sends(ka, kp, kq, own=False):
        key = (ka, kp, kq, 0)
        out = []
        if isinstance(kp, int) and kp == 0 and isinstance(kq, int) and kq == 0:
            out += [
                copy(key, (0, m, n, 0), b_sem.at[ka, m, n], own)
                for m in range(p_n) for n in range(q_n) if m or n
            ]
        out += [
            copy(key, (0, 0, 0, n), c_sem.at[ka * p_n + kp, kq, n], own) for n in range(1, c_n)
        ]
        return out

    def firsts():
        return [copy((0, 0, 0, 0), (n, 0, 0, 0), a_sem.at[n], True) for n in range(1, a_n)]

    def over_a(fn):
        if a_n <= 8:
            for ka in range(1, a_n):
                fn(ka)
        elif a_n > 1:
            lax.fori_loop(1, a_n, lambda ka, _: (fn(ka), 0)[1], 0)

    def relay(ka, kp, kq):
        arrived(ka, kp, kq, 0)
        for cp in sends(ka, kp, kq):
            cp.start()

    for cp in firsts() + sends(0, 0, 0, True) + asked:
        cp.start()
    staged.wait()
    g_out[...] = jnp.swapaxes(g_raw[...], 0, 1)
    for kp in range(1, p_n):
        relay(0, kp, 0)
    for kq in range(1, q_n):
        relay(0, 0, kq)
    over_a(lambda ka: relay(ka, 0, 0))
    for kp in range(1, p_n):
        for kq in range(1, q_n):
            relay(0, kp, kq)

    def last(ka):
        for kp in range(p_n):
            for kq in range(q_n):
                for kc in range(1, c_n):
                    arrived(ka, kp, kq, kc)

    for cp in asked:
        cp.wait()
    noted.wait()
    for n in range(1, b_n):
        noted = pltpu.make_async_copy(near_ref.at[n], near.at[n], near_sem.at[0, 0])
        noted.start()
        noted.wait()
    for cp in across:
        cp.wait()
    mine.wait()
    last(0)
    meanwhile()
    over_a(lambda ka: [relay(ka, kp, 0) for kp in range(1, p_n)])
    over_a(lambda ka: [relay(ka, 0, kq) for kq in range(1, q_n)])
    over_a(lambda ka: [relay(ka, kp, kq) for kp in range(1, p_n) for kq in range(1, q_n)])
    over_a(last)

    def finish():
        def sent(ka):
            for kp in range(p_n):
                for kq in range(q_n):
                    for cp in sends(ka, kp, kq):
                        cp.wait_send()

        sent(0)
        over_a(sent)
        for cp in firsts():
            cp.wait_send()

    return finish


def lay_keys(dims, keys, start, all_ref, block_of, many, strip):
    a_n, b_n, g_n, c_n = dims
    g = lax.axis_index("heads") // c_n
    parts = all_ref.shape[2] // strip

    def lay(at, k, h):
        nonlocal start
        for c1 in range(c_n):
            keys[start : start + strip, :] = all_ref[
                at, other(g, k, g_n) * c_n + c1, h * strip : (h + 1) * strip, :
            ]
            start += strip

    blocks = [block_of(p) for p in range(many)]
    for h in range(parts):
        for at in blocks:
            for k in range(1, g_n):
                lay(at, k, h)
    for h in range(parts):
        for at in blocks:
            lay(at, 0, h)


def attend(
    dims, scale, width, finish, near_ref, all_ref, q_ref, g_ref, o_ref, dq_ref, out_ref,
    keys, own_scores, own_grad, keys_t, probs, grads, o_rows, sent, kept, sent_in, kept_in, g_out, g_in, sums, x_out, z_out, z_in,
    c_sem, g_sem, x_sem, z_sem, *x_in,
):
    a_n, b_n, g_n, c_n = dims
    me = place(dims)
    a, b, g, c = me
    chosen = near_ref.shape[2]
    heads, tokens, value_width = g_ref.shape
    key_width, columns = q_ref.shape
    strips, _, strip, _ = kept.shape
    parts = strips // (chosen + 1)
    many = parts * chosen
    block = own_scores.shape[0]
    before = keys.shape[0] - block
    f32, bf16 = jnp.float32, jnp.bfloat16
    across = (((1,), (1,)), ((), ()))
    down = (((0,), (0,)), ((), ()))
    share = strip * c_n
    runs = [(n * chosen, (n + 1) * chosen) for n in range(parts)]
    own = (many, strips)

    def copy(src, dst, sems, there):
        a2, b2, g2, c2 = there
        return pltpu.make_async_remote_copy(
            src_ref=src,
            dst_ref=dst,
            send_sem=sems.at[0],
            recv_sem=sems.at[1],
            device_id=(g2 * c_n + c2, a2 * b_n + b2),
            device_id_type=MESH,
        )

    def to_c(n, k):
        c2 = other(c, k, c_n)
        first, last = (runs + runs + [own, own])[n]
        at = pl.ds(first, last - first)
        if n < parts or n == 2 * parts:
            src, dst = sent.at[at, :, c2], sent_in.at[k, at]
        else:
            src, dst = kept.at[at, c2], kept_in.at[k, at]
        return copy(src, dst, c_sem.at[n, k], (a, b, g, c2))

    def to_g(n, k):
        first, last = (runs + [own])[n]
        at = pl.ds(first, last - first)
        return copy(g_out.at[k, at], g_in.at[k, at], g_sem.at[n, k], (a, b, other(g, k, g_n), c))

    def to_x(n, k):
        src, dst = x_out.at[pl.ds(n * chosen, chosen)], x_in[n].at[k, pl.ds(1, chosen)]
        return copy(src, dst, x_sem.at[n, k], (a, other(b, k, b_n), g, c))

    def to_z(h, k):
        return copy(z_out.at[h, k], z_in.at[h, k], z_sem.at[h, k], (along(a, k, a_n), b, g, c))

    for h in range(parts):
        sums[h, 0] = jnp.zeros(sums.shape[2:], f32)
        for k in range(1, b_n):
            x_in[h][k, 0] = jnp.zeros(x_in[h].shape[2:], bf16)

    lay_keys(dims, keys, 0, all_ref, lambda p: near_ref[0, 0, p], chosen, strip)

    def rows_of(n):
        return g_ref[n // tokens : (n + width) // tokens].reshape(width, value_width)

    for n in range(0, columns, width):
        at = slice(n, n + width)
        scores = jnp.dot(keys[:before, :], q_ref[:, at], preferred_element_type=f32)
        near_scores = own_scores[:, at]
        top = jnp.maximum(
            jnp.max(scores, axis=0, keepdims=True), jnp.max(near_scores, axis=0, keepdims=True)
        )
        weights = jnp.exp((scores - top) * scale)
        near_weights = jnp.exp((near_scores - top) * scale)
        norm = 1.0 / (
            jnp.sum(weights, axis=0, keepdims=True) + jnp.sum(near_weights, axis=0, keepdims=True)
        )
        grad_prob = lax.dot_general(
            keys[:before, :value_width], rows_of(n), across, preferred_element_type=f32
        )
        near_grad = own_grad[:, at]
        delta = norm * (
            jnp.sum(weights * grad_prob, axis=0, keepdims=True)
            + jnp.sum(near_weights * near_grad, axis=0, keepdims=True)
        )
        probs[:before, at] = (weights * norm).astype(bf16)
        probs[before:, at] = (near_weights * norm).astype(bf16)
        grads[:before, at] = (weights * (norm * scale) * (grad_prob - delta)).astype(bf16)
        grads[before:, at] = (near_weights * (norm * scale) * (near_grad - delta)).astype(bf16)

    def contribution(at):
        total = lax.dot_general(grads[at, :], q_ref[...], across, preferred_element_type=f32)
        value = jnp.dot(
            probs[at, :], g_ref[...].reshape(columns, value_width), preferred_element_type=f32
        )
        total = jnp.concatenate([total[:, :value_width] + value, total[:, value_width:]], axis=1)
        return total.astype(bf16)

    def hand_over(n):
        for k in range(1, c_n):
            to_c(n, k).start()

    def contribute_sent(h):
        high = chosen * (g_n - 1) * share
        first, last = runs[h]
        sent[first:last] = contribution(slice(h * high, (h + 1) * high)).reshape(
            (chosen,) + sent.shape[1:]
        )
        hand_over(h)

    def contribute_kept(h):
        first, last = runs[h]
        base = before - many * share
        kept[first:last] = contribution(slice(base + first * share, base + last * share)).reshape(
            (chosen,) + kept.shape[1:]
        )
        hand_over(parts + h)

    def contribute_own():
        total = contribution(slice(before, before + block))
        split = parts * (g_n - 1) * share
        sent[many:] = total[:split].reshape((parts,) + sent.shape[1:])
        kept[many:] = total[split:].reshape((parts,) + kept.shape[1:])
        hand_over(2 * parts)
        hand_over(2 * parts + 1)

    def take_over(n):
        for k in range(1, c_n):
            to_c(n, k).wait_recv()

    def to_groups(n):
        take_over(n if n < parts else 2 * parts)
        for m in range(1, g_n):
            for u in range(*(runs + [own])[n]):
                total = sent[u, m - 1, c].astype(f32)
                for k in range(1, c_n):
                    total += sent_in[k, u, m - 1].astype(f32)
                g_out[m, u] = total.astype(bf16)
            to_g(n, m).start()

    def from_groups(n):
        take_over(parts + n if n < parts else 2 * parts + 1)
        for k in range(1, g_n):
            to_g(n, k).wait_recv()

    def head_sum(u):
        total = kept[u, c].astype(f32)
        for k in range(1, c_n):
            total += kept_in[k, u].astype(f32)
        for k in range(1, g_n):
            total += g_in[k, u].astype(f32)
        return total

    def to_row(n):
        from_groups(n)
        for u in range(*runs[n]):
            total = head_sum(u)
            sums[n, u % chosen + 1] = total
            x_out[u] = total.astype(bf16)
        for k in range(1, b_n):
            to_x(n, k).start()

    def outputs(n):
        o_rows[n : n + width, :] = lax.dot_general(
            probs[:, n : n + width], keys[:, :value_width], down, preferred_element_type=f32
        ).astype(bf16)
        dq = jnp.dot(keys_t[...], grads[:, n : n + width], preferred_element_type=f32).astype(bf16)
        for m in range(width // tokens):
            dq_ref[n // tokens + m] = dq[:, m * tokens : (m + 1) * tokens]

    def slot(row, wanted):
        at = 0
        for p in range(chosen):
            at = jnp.where(row(p) == wanted, p + 1, at)
        return at

    def dense(h, a1):
        wanted = a1 * b_n + b
        total = sums[h, slot(lambda p: near_ref[0, 0, p], wanted)]
        for k in range(1, b_n):
            total += x_in[h][k, slot(lambda p: near_ref[k, 0, p], wanted)].astype(f32)
        return total

    def to_holders(h):
        for k in range(1, b_n):
            to_x(h, k).wait_recv()

        def send(k):
            z_out[h, k] = dense(h, along(a, k, a_n)).astype(bf16)
            to_z(h, k).start()

        looped(1, a_n, send, True)
        out_ref[h * strip : (h + 1) * strip, :] = dense(h, a)

    starts = list(range(0, columns, width))
    cuts = [len(starts) * n // (parts + 2) for n in range(parts + 3)]

    def some_outputs(n):
        for m in starts[cuts[n] : cuts[n + 1]]:
            outputs(m)

    for n in range(parts):
        contribute_sent(n)
    to_groups(0)
    for n in range(parts):
        contribute_kept(n)
        if n + 1 < parts:
            to_groups(n + 1)
    keys_t[...] = keys[...].T
    to_row(0)
    contribute_own()
    for n in range(1, parts):
        to_row(n)
    to_groups(parts)
    for n in range(parts):
        to_holders(n)
        if n == 0:
            some_outputs(0)
    some_outputs(1)
    some_outputs(2)
    some_outputs(parts + 1)
    part = 8 if heads % 8 == 0 else heads
    for h in range(0, heads, part):
        o_ref[:, h : h + part, :] = jnp.swapaxes(
            o_rows[h * tokens : (h + part) * tokens, :].reshape(part, tokens, value_width), 0, 1
        )
    from_groups(parts)
    for h in range(parts):
        out_ref[h * strip : (h + 1) * strip, :] += head_sum(many + h)
    finish()
    for n in range(2 * parts + 2):
        for k in range(1, c_n):
            to_c(n, k).wait_send()
    for n in range(parts + 1):
        for k in range(1, g_n):
            to_g(n, k).wait_send()
        if n < parts:
            for k in range(1, b_n):
                to_x(n, k).wait_send()
    for h in range(parts):
        looped(1, a_n, lambda k: to_z(h, k).wait_send())

        def take(k):
            to_z(h, k).wait_recv()
            out_ref[h * strip : (h + 1) * strip, :] += z_in[h, k].astype(f32)

        looped(1, a_n, take)


def layer_kernel(
    dims, scale, width, sel_raw, own_ref, q_raw, g_in, o_ref, dq_ref, out_ref,
    pieces, g_rows, q_cols, near_raw, near, *refs,
):
    keys, own_scores, own_grad = refs[9:12]
    block = own_scores.shape[0]
    before = keys.shape[0] - block
    tokens, value_width = g_rows.shape[1:]

    def own_block():
        at = lax.axis_index("seq")
        lay_keys(dims, keys, before, pieces, lambda p: at, 1, refs[17].shape[2])
        for n in range(0, q_cols.shape[1], width):
            rows = g_rows[n // tokens : (n + width) // tokens].reshape(width, value_width)
            own_scores[:, n : n + width] = jnp.dot(
                keys[before:, :], q_cols[:, n : n + width], preferred_element_type=jnp.float32
            )
            own_grad[:, n : n + width] = lax.dot_general(
                keys[before:, :value_width], rows, (((1,), (1,)), ((), ())),
                preferred_element_type=jnp.float32,
            )

    finish = gather(
        dims, own_block, own_ref, g_in, q_raw, sel_raw, pieces, g_rows, q_cols, near_raw, near,
        *refs[:9],
    )
    attend(
        dims, scale, width, finish, near, pieces, q_cols, g_rows, o_ref, dq_ref, out_ref,
        *refs[9:],
    )


def layer(selected, latents, queries, grad_out, dims):
    a_n, b_n, g_n, c_n = dims
    n_s, n_h = a_n * b_n, g_n * c_n
    heads, key_width, tokens = queries.shape
    value_width = grad_out.shape[2]
    columns = heads * tokens
    count = selected.shape[1] + 1
    rows = latents.shape[1]
    keys = count * rows * n_h
    one = (rows, key_width)
    parts = 2 if rows % 32 == 0 else 1
    strips = parts * count
    strip = (rows // parts, key_width)
    dma = pltpu.SemaphoreType.DMA
    half = functools.partial(pltpu.VMEM, dtype=jnp.bfloat16)
    width = tokens * (4 if heads % 4 == 0 else 1)
    return pl.pallas_call(
        functools.partial(layer_kernel, dims, key_width ** (-0.5), width),
        out_shape=(
            half((tokens, heads, value_width)),
            half((heads, key_width, tokens)),
            pltpu.VMEM(one, jnp.float32),
        ),
        in_specs=[pl.BlockSpec(memory_space=HBM)] * 4,
        out_specs=[pl.BlockSpec(memory_space=VMEM)] * 3,
        scratch_shapes=[
            half((n_s, n_h) + one),
            half((heads, tokens, value_width)),
            half((key_width, columns)),
            pltpu.VMEM((b_n,) + selected.shape, selected.dtype),
            SMEM((b_n,) + selected.shape, selected.dtype),
            half(grad_out.shape),
            dma,
            dma((heads,)),
            dma,
            dma((a_n,)),
            dma((a_n, g_n, b_n)),
            dma((a_n * g_n, b_n, c_n)),
            dma((n_s, n_h)),
            dma((2, b_n)),
            half((keys, key_width)),
            pltpu.VMEM((rows * n_h, columns), jnp.float32),
            pltpu.VMEM((rows * n_h, columns), jnp.float32),
            half((key_width, keys)),
            half((keys, columns)),
            half((keys, columns)),
            half((columns, value_width)),
            half((strips, g_n - 1, c_n) + strip),
            half((strips, c_n) + strip),
            half((c_n, strips, g_n - 1) + strip),
            half((c_n, strips) + strip),
            half((g_n, strips) + strip),
            half((g_n, strips) + strip),
            pltpu.VMEM((parts, count) + strip, jnp.float32),
            half((strips,) + strip),
            half((parts, a_n) + strip),
            half((parts, a_n) + strip),
            dma((2 * parts + 2, c_n, 2)),
            dma((parts + 1, g_n, 2)),
            dma((parts, b_n, 2)),
            dma((parts, a_n, 2)),
        ] + [half((b_n, count) + strip)] * parts,
        compiler_params=pltpu.CompilerParams(
            collective_id=0, has_side_effects=True, vmem_limit_bytes=67043328 - 5500000
        ),
        name="layer",
    )(selected, latents, queries, grad_out)


def hand_out_kernel(*refs):
    n = (len(refs) - 1) // 2
    copies = [pltpu.make_async_copy(refs[k], refs[n + k], refs[-1].at[k]) for k in range(n)]
    for cp in copies:
        cp.start()
    for cp in copies:
        cp.wait()


def hand_out(arrays):
    return pl.pallas_call(
        hand_out_kernel,
        out_shape=[jax.ShapeDtypeStruct(x.shape, x.dtype) for x in arrays],
        in_specs=[pl.BlockSpec(memory_space=VMEM) for _ in arrays],
        out_specs=[pl.BlockSpec(memory_space=HBM) for _ in arrays],
        scratch_shapes=[pltpu.SemaphoreType.DMA((len(arrays),))],
        compiler_params=pltpu.CompilerParams(vmem_limit_bytes=16 * 1024 * 1024),
        name="hand_out",
    )(*arrays)


def shards(dims, queries, latents, grad_out, selected):
    assert latents.shape[0] == 1
    output, grad_query, latent_grad = hand_out(
        layer(selected, latents, jnp.transpose(queries, (1, 2, 0)), grad_out, dims)
    )
    return output, jnp.transpose(grad_query, (2, 0, 1)), latent_grad[None]


def solution(mesh):
    n_h, n_s = mesh.shape["heads"], mesh.shape["seq"]
    b_n = 2 if n_s % 2 == 0 else 1
    c_n = 2 if n_h % 2 == 0 else 1
    dims = (n_s // b_n, b_n, n_h // c_n, c_n)
    in_specs = (
        P("seq", "heads", None),
        P("seq", "heads", None),
        P("seq", "heads", None),
        P("seq", None),
    )
    out_specs = (P("seq", "heads", None), P("seq", "heads", None), P("seq", "heads", None))
    return jax.shard_map(
        functools.partial(shards, dims),
        mesh=mesh, in_specs=in_specs, out_specs=out_specs, check_vma=False,
    )
```
